128 devices in a mesh: layer: 4 (over x), row: 16 (over z, y), col: 2 (over core).
Axes of the slice: x: 4, y: 4, z: 4, core: 2. Of those that a mesh axis runs over, the one named last changes fastest.
Arguments:
- density: bfloat16 [8192, 8192], P('row', 'col'), may hold values from -0.5 to 1.5
- pattern: int32 [64, 64], P('row', 'col'), may hold values from 0 to 1, as said below
- holder: int32 [4096, 1], P(('layer', 'row', 'col')), may hold values from 0 to 31; in each aligned block of 32 rows (0 to 31, 32 to 63, ...) at most 2 rows name the same one
- slot_index: int32 [4096], P(('layer', 'row', 'col')), may hold values from 0 to 31
- atom_index: int32 [4096], P(('layer', 'row', 'col')), may hold values from 0 to 7
- derivative: bfloat16 [4096, 3, 128, 128], P(('layer', 'row', 'col')), may hold values from -1.1953125 to 1.1953125
Outputs:
- forces: float32 [3, 1024], P(None, ('layer', 'row', 'col'))
The draws below stay inside these ranges and needn't reach their ends.
Inputs may be any that keep to these rules, and one draw needn't show every extreme that they name: `pattern`: the blocks held by one (row, col) grid position form a tile of 4 x 32; in some tile every block is 1. Among the derivative blocks of one device no holder is named more than 2 times, a bound that some block reaches; every holder is named on some device.
All inputs are finite; a program needn't handle non-finite values.
Results may differ from the reference program's by a relative error of at most 0.015.
Values may be sent and summed in bfloat16 or wider, within the bound.
A program may use at most 128 MiB of HBM per device.

```python
import math
import jax
import jax.numpy as jnp
import numpy as np
from jax import lax

BS = 128
BLK = 4
DER_DEV = 32
ATOM_DEV = 8
NB = 64
N = 8192
TC = 32
HOLD = 32
CAP = 2
ENTRIES = 4096
ATOMS = 1024
N_LAYER = 4
N_ROW = 16
N_COL = 2
DEVICES = 128


def draw_density(key, part):
    first_key = jax.random.fold_in(key, 0)
    spread = 0.7 / math.sqrt(N)
    random_part = jax.random.normal(first_key, (N, N), jnp.float32)
    random_part = jnp.clip(random_part, -4.0, 4.0)
    return (0.5 * jnp.eye(N, dtype=jnp.float32) + spread * random_part).astype(jnp.bfloat16)


def draw_pattern(key, part):
    level_key, dense_key, entry_key = jax.random.split(jax.random.fold_in(key, 17), 3)
    levels = jax.random.randint(level_key, (N_ROW, N_COL), 1, 5, dtype=jnp.int32)
    dense_tile = jax.random.randint(dense_key, (), 0, N_ROW * N_COL, dtype=jnp.int32)
    tile_ids = jnp.arange(N_ROW * N_COL, dtype=jnp.int32).reshape(N_ROW, N_COL)
    levels = jnp.where(tile_ids == dense_tile, 4, levels)
    per_block = jnp.repeat(jnp.repeat(levels, BLK, axis=0), TC, axis=1)
    entries = jax.random.randint(entry_key, (NB, NB), 0, 4, dtype=jnp.int32)
    return (entries < per_block).astype(jnp.int32)


def plant(values, own_key, least, largest):
    dims = values.shape
    place = [jax.random.randint(jax.random.fold_in(own_key, axis), (), 0, dims[axis]) for axis in range(len(dims))]
    values = values.at[tuple(place)].set(least)
    longest = dims.index(max(dims))
    place[longest] = (place[longest] + 1) % dims[longest]
    return values.at[tuple(place)].set(largest)


def level_of(key, extent, pieces, least, top_value):
    def one(dim, shards_of):
        draws = jax.random.uniform(jax.random.fold_in(jax.random.fold_in(key, 6), dim), (shards_of,), jnp.float32, least / len(pieces), top_value / len(pieces))
        return jnp.repeat(jnp.exp(draws), extent[dim] // shards_of).reshape((-1,) + (1,) * (len(extent) - dim - 1))

    loudness = one(*pieces[0])
    for cut in pieces[1:]:
        loudness = loudness * one(*cut)
    return loudness


def deal_out(rng, own, number, rows, count, top, reach, lean):
    order = jax.random.permutation(rng, count)
    crowded, ordinary = shares(count, rows * top, reach, lean, True), shares(count, rows * top, reach, lean, False)
    places = jnp.arange(count)

    def named(lengths, turn):
        used = int((lengths > 0).sum())
        fixed = max(1, used // 4)
        shifted = fixed + (places - fixed + turn * (used - fixed)) % max(1, count - fixed)
        return jnp.zeros((count,), jnp.int32).at[order[jnp.where(places < fixed, places, shifted)]].set(jnp.asarray(lengths, jnp.int32))

    lengths = jnp.where(number % 4 == 0, named(crowded, number // 4), named(ordinary, number - number // 4 - 1))
    mixed = jax.random.permutation(jax.random.fold_in(own, 3), count)
    giver, taker = mixed[0:count // 2 * 2:2], mixed[1:count // 2 * 2:2]
    room = jnp.minimum(lengths[giver] - 1, reach - lengths[taker]) // 2
    room = jnp.where((giver == order[0]) | (taker == order[0]) | (lengths[taker] == 0), 0, jnp.maximum(room, 0))
    shifted = jax.random.randint(jax.random.fold_in(own, 4), (count // 2,), 0, 1 << 20) % (room + 1)
    lengths = lengths.at[giver].add(-shifted).at[taker].add(shifted)
    items = jnp.searchsorted(jnp.cumsum(lengths), jnp.arange(rows * top), side="right").astype(jnp.int32)
    grid = items.reshape(top, rows).T
    grid = grid[jax.random.permutation(jax.random.fold_in(own, 1), rows)]
    turn = jax.random.randint(jax.random.fold_in(own, 2), (rows, 1), 0, top)
    return jnp.take_along_axis(grid, (jnp.arange(top)[None, :] + turn) % top, axis=1)


def shares(count, total, limit, skew, full):
    weights = [(1 << 20) // math.isqrt(standing ** skew) + 1 for standing in range(1, count + 1)]
    largest = limit if full else min(limit, max(-(-total // count), total * weights[0] // sum(weights)))
    least = 1 if total - largest >= count - 1 else 0
    holding, rest = [largest] + [least] * (count - 1), total - largest - least * (count - 1)
    while rest > 0:
        free = [i for i in range(1, count) if holding[i] < largest] or [i for i in range(1, count) if holding[i] < limit]
        pool, remaining = sum([weights[i] for i in free]), rest
        for i in free:
            more = min(limit - holding[i], max(1, remaining * weights[i] // pool), rest)
            holding[i] = holding[i] + more
            rest = rest - more
    return np.array(holding)


def scatter_about(key, extent, scale, limit, pieces=(), kind=jnp.bfloat16):
    gain = level_of(key, extent, pieces, -0.22, 0.18) if pieces else 1.0
    drawn = jax.random.normal(key, extent, jnp.float32) * scale * gain
    return jnp.minimum(jnp.maximum(drawn, -limit), limit).astype(kind)


def setup_inputs(seed: int = 0) -> dict:
    splits = jax.random.split(jax.random.key(seed), 7)
    density = draw_density(jax.random.fold_in(splits[6], 71), 0)
    pattern = draw_pattern(jax.random.fold_in(splits[6], 71), 0)
    holder_keys = jax.random.split(jax.random.fold_in(splits[2], 1), ENTRIES // DER_DEV)
    holder_turns = jax.random.permutation(jax.random.fold_in(splits[2], 3), ENTRIES // DER_DEV)
    holder = jax.vmap(lambda own, number: deal_out(jax.random.fold_in(splits[2], 2), own, number, DER_DEV, N_ROW * N_COL, 1, CAP, 2))(holder_keys, holder_turns).reshape((ENTRIES, 1))
    slot_index = plant(jax.random.randint(splits[3], (ENTRIES,), 0, HOLD), jax.random.fold_in(splits[3], 1), 0, HOLD - 1).astype(jnp.int32)
    atom_index = plant(jax.random.randint(splits[4], (ENTRIES,), 0, ATOM_DEV), jax.random.fold_in(splits[4], 1), 0, ATOM_DEV - 1).astype(jnp.int32)
    derivative = scatter_about(splits[5], (ENTRIES, 3, BS, BS), 0.2, 1.1953125, ((0, 128),))
    return {"density": density, "pattern": pattern, "holder": holder, "slot_index": slot_index, "atom_index": atom_index, "derivative": derivative}


def block_filter(matrix, kept_blocks):
    blocked = matrix.reshape(NB, BS, NB, BS)
    return jnp.where(kept_blocks[:, None, :, None], blocked, jnp.zeros_like(blocked)).reshape(N, N)


def reference(density, pattern, holder, slot_index, atom_index, derivative):
    block_ids = jnp.arange(NB, dtype=jnp.int32)
    kept_blocks = (pattern == 1) | (block_ids[:, None] == block_ids[None, :])
    filtered = block_filter(density, kept_blocks)
    square = jnp.dot(filtered, filtered, preferred_element_type=jnp.float32).astype(jnp.bfloat16)
    cube = jnp.dot(square, filtered, preferred_element_type=jnp.float32)
    purified = block_filter(3.0 * square.astype(jnp.float32) - 2.0 * cube, kept_blocks).astype(jnp.bfloat16)
    blocked = purified.reshape(NB, BS, NB, BS)
    col_blocks = NB // N_COL
    owners = jnp.arange(ENTRIES, dtype=jnp.int32) // DER_DEV
    layer_ids = owners // (N_ROW * N_COL)
    holders = holder[:, 0]
    block_row = (holders // N_COL) * BLK + layer_ids * (BLK // N_LAYER) + slot_index // col_blocks
    block_col = (holders % N_COL) * col_blocks + slot_index % col_blocks

    def per_owner(inputs):
        rows_here, cols_here, atoms_here, deriv_here = inputs
        picked = blocked[rows_here, :, cols_here, :]
        contrib = jnp.einsum("eij,exij->xe", picked.astype(jnp.float32), deriv_here.astype(jnp.float32), precision=lax.Precision.HIGHEST)
        atom_hot = (atoms_here[:, None] == jnp.arange(ATOM_DEV, dtype=jnp.int32)[None, :]).astype(jnp.float32)
        return -2.0 * jnp.dot(contrib, atom_hot, precision=lax.Precision.HIGHEST)

    stacked = lax.map(per_owner, (block_row.reshape(DEVICES, DER_DEV), block_col.reshape(DEVICES, DER_DEV), atom_index.reshape(DEVICES, DER_DEV), derivative.reshape(DEVICES, DER_DEV, 3, BS, BS)))
    return jnp.transpose(stacked, (1, 0, 2)).reshape(3, ATOMS)
```

```python
import jax
import jax.numpy as jnp
from jax import lax
from jax.sharding import Mesh, PartitionSpec as P

BS = 128
ATOM_DEV = 8


def kept_of(pattern, grid_row, grid_col):
    row_blocks, col_blocks = pattern.shape
    global_rows = grid_row * row_blocks + jnp.arange(row_blocks, dtype=jnp.int32)
    global_cols = grid_col * col_blocks + jnp.arange(col_blocks, dtype=jnp.int32)
    return (pattern == 1) | (global_rows[:, None] == global_cols[None, :])


def block_filter(matrix, kept_blocks):
    count_rows, count_cols = kept_blocks.shape
    blocked = matrix.reshape(count_rows, BS, count_cols, BS)
    return jnp.where(kept_blocks[:, None, :, None], blocked, jnp.zeros_like(blocked)).reshape(
        matrix.shape
    )


def purify(filtered, kept_blocks):
    x = lax.axis_index("layer")
    bf = jnp.bfloat16
    right = lax.dynamic_slice_in_dim(filtered, x * 1024, 1024, 1)
    right = lax.all_gather(right, "z", axis=0, tiled=True)
    rows = lax.dynamic_slice_in_dim(filtered, x * BS, BS, 0)
    piece = rows.reshape(BS, 2, 4, 512).transpose(2, 0, 1, 3).reshape(4, BS, 1024)
    piece = lax.all_to_all(piece, "y", 0, 0, tiled=True)
    left = lax.all_gather(piece, "layer", axis=0, tiled=False)
    left = lax.all_gather(left, "col", axis=0, tiled=False)
    left = left.transpose(2, 1, 3, 0, 4).reshape(2048, 2048)

    def product(factor):
        partial = jnp.dot(left, factor, preferred_element_type=jnp.float32).astype(bf)
        return lax.psum_scatter(partial, "y", scatter_dimension=0, tiled=True)

    square = product(right)
    cube = product(lax.all_gather(square, "z", axis=0, tiled=True))
    kept = lax.dynamic_slice_in_dim(kept_blocks, x * 8, 8, 1)
    purified = block_filter(
        3.0 * square.astype(jnp.float32) - 2.0 * cube.astype(jnp.float32), kept
    ).astype(bf)
    blocks = purified.reshape(4, BS, 8, BS).transpose(0, 2, 1, 3)
    return lax.all_to_all(blocks, "layer", 0, 0, tiled=True).reshape(32, BS, BS)


def select(indices, blocks):
    hot = indices[:, None] == jnp.arange(blocks.shape[0], dtype=jnp.int32)[None, :]
    flat = jnp.dot(hot.astype(blocks.dtype), blocks.reshape(blocks.shape[0], BS * BS))
    return flat.reshape(-1, BS, BS)


def shards(density, pattern, holder, slot_index, atom_index, derivative):
    grid_row = lax.axis_index("z") * 4 + lax.axis_index("y")
    kept_blocks = kept_of(pattern, grid_row, lax.axis_index("col"))
    held_blocks = purify(block_filter(density, kept_blocks), kept_blocks)
    holders_total = 32
    capacity = 2
    targets = holder[:, 0]
    entries = jnp.arange(targets.shape[0], dtype=jnp.int32)
    earlier = (targets[:, None] == targets[None, :]) & (entries[None, :] < entries[:, None])
    rank_values = jnp.sum(earlier.astype(jnp.int32), axis=1)
    positions = targets * capacity + rank_values
    position_hot = (
        positions[None, :] == jnp.arange(holders_total * capacity, dtype=jnp.int32)[:, None]
    )
    requests = jnp.sum(jnp.where(position_hot, slot_index[None, :], 0), axis=1).reshape(
        holders_total, capacity
    )
    axes = ("z", "y", "col")
    asked = lax.all_to_all(requests, axes, split_axis=0, concat_axis=0, tiled=True).reshape(-1)
    fetched = select(asked, held_blocks).reshape(holders_total, capacity, BS, BS)
    returned = lax.all_to_all(fetched, axes, split_axis=0, concat_axis=0, tiled=True)
    arrived = select(positions, returned.reshape(holders_total * capacity, BS, BS))
    contrib = jnp.einsum("eij,exij->xe", arrived, derivative, preferred_element_type=jnp.float32)
    atom_hot = (atom_index[:, None] == jnp.arange(ATOM_DEV, dtype=jnp.int32)[None, :]).astype(
        jnp.float32
    )
    return -2.0 * jnp.dot(contrib, atom_hot, precision=lax.Precision.HIGHEST)


def solution(mesh):
    split = Mesh(mesh.devices.reshape(4, 4, 4, 2), ("layer", "z", "y", "col"))
    every = ("layer", "z", "y", "col")
    return jax.shard_map(
        shards,
        mesh=split,
        in_specs=(
            P(("z", "y"), "col"),
            P(("z", "y"), "col"),
            P(every, None),
            P(every),
            P(every),
            P(every, None, None, None),
        ),
        out_specs=P(None, every),
        check_vma=False,
    )
```

```python
import jax
import jax.numpy as jnp
from jax import lax
from jax.experimental import pallas as pl
from jax.experimental.pallas import tpu as pltpu
from jax.sharding import Mesh, PartitionSpec as P

BS = 128
ATOM_DEV = 8
CHUNKS = 4
WIDE = 256
F32 = jnp.float32
BF16 = jnp.bfloat16
MESH = pl.DeviceIdType.MESH
COPIES = 130


class Links:
    def __init__(self, place, send_sems, recv_sems):
        self.place, self.send_sems, self.recv_sems = place, send_sems, recv_sems
        self.started = []
        self.count = 0

    def copy(self, src, dst, axis, step):
        number, self.count = self.count, self.count + 1
        length = 2 if axis == "col" else 4
        made = pltpu.make_async_remote_copy(
            src_ref=src,
            dst_ref=dst,
            send_sem=self.send_sems.at[number],
            recv_sem=self.recv_sems.at[number],
            device_id={axis: lax.rem(self.place[axis] + step + length, length)},
            device_id_type=MESH,
        )
        made.start()
        self.started.append(made)
        return made


class Ring:
    def __init__(self, links, axis, slot):
        self.links, self.axis, self.slot = links, axis, slot
        self.own = links.place[axis]

    def start(self):
        mine = self.slot(self.own)
        self.up = self.links.copy(mine, mine, self.axis, 1)
        self.down = self.links.copy(mine, mine, self.axis, -1)

    def forward(self):
        half = self.slot(self.own).shape[0] // 2
        self.up.wait_recv()
        lower = self.slot(lax.rem(self.own + 3, 4)).at[pl.ds(0, half)]
        self.up_half = self.links.copy(lower, lower, self.axis, 1)
        self.down.wait_recv()
        upper = self.slot(lax.rem(self.own + 1, 4)).at[pl.ds(half, half)]
        self.down_half = self.links.copy(upper, upper, self.axis, -1)

    def finish(self):
        self.up_half.wait_recv()
        self.down_half.wait_recv()


def purify_kernel(
    pattern, density, held_out,
    rows_in, cols_in, left, left_send, left_pass, right, square, part, sums_send, sums_recv, pure, held,
    in_sems, send_sems, recv_sems,
):
    x, z, y, c = (lax.axis_index(a) for a in ("layer", "z", "y", "col"))
    place = {"layer": x, "z": z, "y": y, "col": c}
    links = Links(place, send_sems, recv_sems)
    load_rows = pltpu.make_async_copy(
        density.at[pl.ds(pl.multiple_of(x * BS, BS), BS), :], rows_in, in_sems.at[0]
    )
    load_cols = pltpu.make_async_copy(
        density.at[:, pl.ds(pl.multiple_of(x * 1024, 1024), 1024)], cols_in, in_sems.at[1]
    )
    load_rows.start()
    load_cols.start()
    barrier = pltpu.get_barrier_semaphore()
    greeted = 0
    for axis, steps in (("y", (1, 3)), ("z", (1, 3)), ("layer", (1, 2, 3)), ("col", (1,))):
        length = 2 if axis == "col" else 4
        for step in steps:
            pl.semaphore_signal(
                barrier, inc=1, device_id={axis: lax.rem(place[axis] + step, length)},
                device_id_type=MESH,
            )
            greeted += 1

    def kept(row_block, col_block):
        inside = pattern[row_block, col_block] == 1
        return inside | ((z * 4 + y) * 4 + row_block == c * 32 + col_block)

    load_rows.wait()
    for b in range(32):
        block = rows_in[:, b * BS : (b + 1) * BS]
        block = jnp.where(kept(x, b), block, jnp.zeros_like(block))
        lane = (b // 16) * 512 + (b % 4) * BS
        left_send[(b % 16) // 4, :, lane : lane + BS] = block
    left[c, y, x] = left_send[y]
    pl.semaphore_wait(barrier, greeted)

    def over(step):
        return lax.rem(y + step, 4)

    y_up = links.copy(left_send.at[over(1)], left.at[c, y, x], "y", 1)
    y_down = links.copy(left_send.at[over(3)], left.at[c, y, x], "y", -1)
    far = left_send.at[over(2)]
    y_up_pass = links.copy(far.at[pl.ds(0, 64)], left_pass.at[0], "y", 1)
    y_down_pass = links.copy(far.at[pl.ds(64, 64)], left_pass.at[1], "y", -1)

    load_cols.wait()
    for b in range(8):
        for r in range(4):
            block = cols_in[r * BS : (r + 1) * BS, b * BS : (b + 1) * BS]
            block = jnp.where(kept(r, x * 8 + b), block, jnp.zeros_like(block))
            lane = (b % 2) * BS
            right[b // 2, z, r * BS : (r + 1) * BS, lane : lane + BS] = block
    rights = [Ring(links, "z", lambda s, j=j: right.at[j, s]) for j in range(CHUNKS)]
    rights[0].start()

    lefts = {}
    crossed = []

    def spread(step):
        lefts[step] = Ring(links, "layer", lambda s: left.at[c, over(step), s])
        lefts[step].start()
        cross(step, 0)

    def cross(step, away):
        piece = left.at[c, over(step), lax.rem(x + away, 4)]
        crossed.append(links.copy(piece, piece, "col", 1))

    spread(0)
    y_up.wait_recv()
    spread(3)
    y_down.wait_recv()
    spread(1)
    y_up_pass.wait_recv()
    y_up_far = links.copy(left_pass.at[0], left.at[c, over(3), x, pl.ds(0, 64)], "y", 1)
    y_down_pass.wait_recv()
    y_down_far = links.copy(left_pass.at[1], left.at[c, over(1), x, pl.ds(64, 64)], "y", -1)
    rights[0].forward()
    rights[1].start()
    y_up_far.wait_recv()
    y_down_far.wait_recv()
    spread(2)
    for turn, step in enumerate((0, 3, 1, 2)):
        lefts[step].forward()
        cross(step, 3)
        cross(step, 1)
        if turn < 3:
            rights[turn + 1].forward()
            if turn < 2:
                rights[turn + 2].start()
    for step in (0, 3, 1, 2):
        lefts[step].finish()
        cross(step, 2)
    for made in crossed:
        made.wait_recv()

    def multiply(j, factor):
        def panel(i, carry):
            d = lax.rem(y + jnp.where(i == 0, 2, jnp.where(i == 1, 1, jnp.where(i == 2, 3, 0))), 4)
            total = jnp.zeros((512, WIDE), F32)
            for k in range(2):
                total += jnp.dot(
                    left[k, d].reshape(512, 1024),
                    factor[j, 2 * k : 2 * k + 2].reshape(1024, WIDE),
                    preferred_element_type=F32,
                )
            part[j, i] = total
            return carry

        lax.fori_loop(0, 4, panel, 0)

    class Sums:
        def __init__(self, j, stage):
            self.j, self.slot = j, stage * CHUNKS + j

        def send(self, n, value, step):
            sums_send[self.slot, n] = value.astype(BF16)
            return links.copy(sums_send.at[self.slot, n], sums_recv.at[self.slot, n], "y", step)

        def start(self):
            j = self.j
            self.made = [
                self.send(0, part[j, 0, 0:256], 1),
                self.send(1, part[j, 0, 256:512], -1),
                self.send(2, part[j, 1, 256:512], 1),
                self.send(3, part[j, 2, 0:256], -1),
            ]

        def combine(self):
            j = self.j
            self.made[0].wait_recv()
            self.made.append(self.send(4, part[j, 1, 0:256] + sums_recv[self.slot, 0].astype(F32), 1))
            self.made[1].wait_recv()
            self.made.append(self.send(5, part[j, 2, 256:512] + sums_recv[self.slot, 1].astype(F32), -1))

        def result(self):
            for n in (2, 3, 4, 5):
                self.made[n].wait_recv()
            halves = []
            for h, (a, b) in enumerate(((3, 4), (2, 5))):
                own = part[self.j, 3, h * 256 : (h + 1) * 256]
                halves.append(
                    own + sums_recv[self.slot, a].astype(F32) + sums_recv[self.slot, b].astype(F32)
                )
            return halves

    squares = [Sums(j, 0) for j in range(CHUNKS)]
    cubes = [Sums(j, 1) for j in range(CHUNKS)]
    gathers = [Ring(links, "z", lambda s, j=j: square.at[j, s]) for j in range(CHUNKS)]
    handed = []

    def first(j):
        rights[j].finish()
        multiply(j, right)
        squares[j].start()

    def squared(j):
        for h, value in enumerate(squares[j].result()):
            square[j, z, h * 256 : (h + 1) * 256] = value.astype(BF16)
        gathers[j].start()

    def second(j):
        gathers[j].finish()
        multiply(j, square)
        cubes[j].start()

    def purified(j):
        for h, value in enumerate(cubes[j].result()):
            for r in range(2):
                row = 2 * h + r
                for b in range(2):
                    lanes = slice(b * BS, (b + 1) * BS)
                    own = square[j, z, row * BS : (row + 1) * BS, lanes].astype(F32)
                    block = 3.0 * own - 2.0 * value[r * BS : (r + 1) * BS, lanes]
                    block = jnp.where(kept(row, x * 8 + j * 2 + b), block, jnp.zeros_like(block))
                    pure[j, row, b] = block.astype(BF16)
        where = x * 8 + j * 2
        for step in (1, 2, 3):
            to = lax.rem(x + step, 4)
            handed.append(links.copy(pure.at[j, to], held.at[pl.ds(where, 2)], "layer", step))
        for b in range(2):
            held[where + b] = pure[j, x, b]

    first(0)
    first(1)
    squares[0].combine()
    first(2)
    squares[1].combine()
    squared(0)
    first(3)
    squares[2].combine()
    squared(1)
    gathers[0].forward()
    squares[3].combine()
    second(0)
    squared(2)
    gathers[1].forward()
    cubes[0].combine()
    second(1)
    squared(3)
    gathers[2].forward()
    cubes[1].combine()
    purified(0)
    second(2)
    gathers[3].forward()
    cubes[2].combine()
    purified(1)
    second(3)
    cubes[3].combine()
    purified(2)
    purified(3)
    for made in handed:
        made.wait_recv()
    held_out[...] = held[...]
    for made in links.started:
        made.wait_send()
    assert links.count == COPIES, links.count


def purify(density, pattern):
    return pl.pallas_call(
        purify_kernel,
        out_shape=jax.ShapeDtypeStruct((32, BS, BS), BF16),
        in_specs=[
            pl.BlockSpec(memory_space=pltpu.SMEM),
            pl.BlockSpec(memory_space=pl.ANY),
        ],
        out_specs=pl.BlockSpec(memory_space=pltpu.VMEM),
        scratch_shapes=[
            pltpu.VMEM((BS, 4096), BF16),
            pltpu.VMEM((512, 1024), BF16),
            pltpu.VMEM((2, 4, 4, BS, 1024), BF16),
            pltpu.VMEM((4, BS, 1024), BF16),
            pltpu.VMEM((2, 64, 1024), BF16),
            pltpu.VMEM((CHUNKS, 4, 512, WIDE), BF16),
            pltpu.VMEM((CHUNKS, 4, 512, WIDE), BF16),
            pltpu.VMEM((CHUNKS, 4, 512, WIDE), F32),
            pltpu.VMEM((2 * CHUNKS, 6, 256, WIDE), BF16),
            pltpu.VMEM((2 * CHUNKS, 6, 256, WIDE), BF16),
            pltpu.VMEM((CHUNKS, 4, 2, BS, BS), BF16),
            pltpu.VMEM((32, BS, BS), BF16),
            pltpu.SemaphoreType.DMA((2,)),
            pltpu.SemaphoreType.DMA((COPIES,)),
            pltpu.SemaphoreType.DMA((COPIES,)),
        ],
        compiler_params=pltpu.CompilerParams(
            collective_id=0, has_side_effects=True, vmem_limit_bytes=56 << 20
        ),
    )(pattern, density)


def select(indices, blocks):
    hot = indices[:, None] == jnp.arange(blocks.shape[0], dtype=jnp.int32)[None, :]
    flat = jnp.dot(hot.astype(blocks.dtype), blocks.reshape(blocks.shape[0], BS * BS))
    return flat.reshape(-1, BS, BS)


def shards(density, pattern, holder, slot_index, atom_index, derivative):
    held_blocks = purify(density, pattern)
    holders_total = 32
    capacity = 2
    targets = holder[:, 0]
    entries = jnp.arange(targets.shape[0], dtype=jnp.int32)
    earlier = (targets[:, None] == targets[None, :]) & (entries[None, :] < entries[:, None])
    rank_values = jnp.sum(earlier.astype(jnp.int32), axis=1)
    positions = targets * capacity + rank_values
    position_hot = (
        positions[None, :] == jnp.arange(holders_total * capacity, dtype=jnp.int32)[:, None]
    )
    requests = jnp.sum(jnp.where(position_hot, slot_index[None, :], 0), axis=1).reshape(
        holders_total, capacity
    )
    axes = ("z", "y", "col")
    asked = lax.all_to_all(requests, axes, split_axis=0, concat_axis=0, tiled=True).reshape(-1)
    fetched = select(asked, held_blocks).reshape(holders_total, capacity, BS, BS)
    returned = lax.all_to_all(fetched, axes, split_axis=0, concat_axis=0, tiled=True)
    arrived = select(positions, returned.reshape(holders_total * capacity, BS, BS))
    contrib = jnp.einsum("eij,exij->xe", arrived, derivative, preferred_element_type=jnp.float32)
    atom_hot = (atom_index[:, None] == jnp.arange(ATOM_DEV, dtype=jnp.int32)[None, :]).astype(
        jnp.float32
    )
    return -2.0 * jnp.dot(contrib, atom_hot, precision=lax.Precision.HIGHEST)


def solution(mesh):
    split = Mesh(mesh.devices.reshape(4, 4, 4, 2), ("layer", "z", "y", "col"))
    every = ("layer", "z", "y", "col")
    return jax.shard_map(
        shards,
        mesh=split,
        in_specs=(
            P(("z", "y"), "col"),
            P(("z", "y"), "col"),
            P(every, None),
            P(every),
            P(every),
            P(every, None, None, None),
        ),
        out_specs=P(None, every),
        check_vma=False,
    )
```

```python
import jax
import jax.numpy as jnp
from jax import lax
from jax.experimental import pallas as pl
from jax.experimental.pallas import tpu as pltpu
from jax.sharding import Mesh, PartitionSpec as P

BS = 128
ATOM_DEV = 8
CHUNKS = 4
WIDE = 256
F32 = jnp.float32
BF16 = jnp.bfloat16
MESH = pl.DeviceIdType.MESH
COPIES = 192


class Links:
    def __init__(self, place, send_sems, recv_sems):
        self.place, self.send_sems, self.recv_sems = place, send_sems, recv_sems
        self.started = []
        self.count = 0

    def copy(self, src, dst, axis, step):
        length = 2 if axis == "col" else 4
        return self.to(src, dst, {axis: lax.rem(self.place[axis] + step + length, length)})

    def to(self, src, dst, device):
        number, self.count = self.count, self.count + 1
        made = pltpu.make_async_remote_copy(
            src_ref=src,
            dst_ref=dst,
            send_sem=self.send_sems.at[number],
            recv_sem=self.recv_sems.at[number],
            device_id=device,
            device_id_type=MESH,
        )
        made.start()
        self.started.append(made)
        return made


class Ring:
    def __init__(self, links, axis, slot):
        self.links, self.axis, self.slot = links, axis, slot
        self.own = links.place[axis]

    def start(self):
        mine = self.slot(self.own)
        self.up = self.links.copy(mine, mine, self.axis, 1)
        self.down = self.links.copy(mine, mine, self.axis, -1)

    def forward(self):
        half = self.slot(self.own).shape[0] // 2
        self.up.wait_recv()
        lower = self.slot(lax.rem(self.own + 3, 4)).at[pl.ds(0, half)]
        self.up_half = self.links.copy(lower, lower, self.axis, 1)
        self.down.wait_recv()
        upper = self.slot(lax.rem(self.own + 1, 4)).at[pl.ds(half, half)]
        self.down_half = self.links.copy(upper, upper, self.axis, -1)

    def finish(self):
        self.up_half.wait_recv()
        self.down_half.wait_recv()


def purify_kernel(
    pattern, density, targets_col, targets_row, slots_row, atoms_col, derivative, forces,
    rows_in, cols_in, left, left_send, left_pass, right, square, part, sums_send, sums_recv, pure, held,
    der, asked_send, asked_recv, asked_rows, spots, asked, spot_of, picked, arrived, contrib,
    in_sems, send_sems, recv_sems,
):
    x, z, y, c = (lax.axis_index(a) for a in ("layer", "z", "y", "col"))
    place = {"layer": x, "z": z, "y": y, "col": c}
    links = Links(place, send_sems, recv_sems)
    load_rows = pltpu.make_async_copy(
        density.at[pl.ds(pl.multiple_of(x * BS, BS), BS), :], rows_in, in_sems.at[0]
    )
    load_cols = pltpu.make_async_copy(
        density.at[:, pl.ds(pl.multiple_of(x * 1024, 1024), 1024)], cols_in, in_sems.at[1]
    )
    load_rows.start()
    load_cols.start()
    load_der = pltpu.make_async_copy(derivative, der, in_sems.at[2])
    load_der.start()
    barrier = pltpu.get_barrier_semaphore()
    others = [(dz, dy, dc) for dz in (2, 1, 3, 0) for dy in (2, 1, 3, 0) for dc in (0, 1)][:-2]
    others.append((0, 0, 1))

    def device(dz, dy, dc):
        return {"z": lax.rem(z + dz, 4), "y": lax.rem(y + dy, 4), "col": lax.rem(c + dc, 2)}

    def holder_of(at):
        return at["z"] * 8 + at["y"] * 2 + at["col"]

    me = z * 8 + y * 2 + c
    greeted = [device(*d) for d in others] + [{"layer": lax.rem(x + step, 4)} for step in (1, 2, 3)]
    for at in greeted:
        pl.semaphore_signal(barrier, inc=1, device_id=at, device_id_type=MESH)

    across = lax.broadcasted_iota(jnp.int32, (32, 32), 1)
    down = lax.broadcasted_iota(jnp.int32, (32, 32), 0)
    earlier = (targets_col[...] == targets_row[...]) & (down < across)
    spot = 2 * targets_row[...] + jnp.sum(jnp.where(earlier, 1, 0), axis=0, keepdims=True)
    spots[...] = jnp.zeros_like(spots)
    spots[0:1, 0:32] = spot
    lane = lax.broadcasted_iota(jnp.int32, (32, BS), 1)
    table = jnp.zeros((32, BS), jnp.int32)
    for k in range(2):
        mine = jnp.where(spot == 2 * down + k, slots_row[...], 0)
        table = jnp.where(lane == k, jnp.sum(mine, axis=1, keepdims=True), table)
    asked_send[...] = jnp.broadcast_to(table[:, None, :], asked_send.shape)
    asked_recv[me] = asked_send[me]

    def kept(row_block, col_block):
        inside = pattern[row_block, col_block] == 1
        return inside | ((z * 4 + y) * 4 + row_block == c * 32 + col_block)

    load_rows.wait()
    for b in range(32):
        block = rows_in[:, b * BS : (b + 1) * BS]
        block = jnp.where(kept(x, b), block, jnp.zeros_like(block))
        lane = (b // 16) * 512 + (b % 4) * BS
        left_send[(b % 16) // 4, :, lane : lane + BS] = block
    left[c, y, x] = left_send[y]
    pl.semaphore_wait(barrier, len(greeted))

    def over(step):
        return lax.rem(y + step, 4)

    y_up = links.copy(left_send.at[over(1)], left.at[c, y, x], "y", 1)
    y_down = links.copy(left_send.at[over(3)], left.at[c, y, x], "y", -1)
    far = left_send.at[over(2)]
    y_up_pass = links.copy(far.at[pl.ds(0, 64)], left_pass.at[0], "y", 1)
    y_down_pass = links.copy(far.at[pl.ds(64, 64)], left_pass.at[1], "y", -1)

    load_cols.wait()
    for b in range(8):
        for r in range(4):
            block = cols_in[r * BS : (r + 1) * BS, b * BS : (b + 1) * BS]
            block = jnp.where(kept(r, x * 8 + b), block, jnp.zeros_like(block))
            lane = (b % 2) * BS
            right[b // 2, z, r * BS : (r + 1) * BS, lane : lane + BS] = block
    requests = []
    for d in others:
        at = device(*d)
        requests.append(links.to(asked_send.at[holder_of(at)], asked_recv.at[me], at))
    rights = [Ring(links, "z", lambda s, j=j: right.at[j, s]) for j in range(CHUNKS)]
    rights[0].start()

    lefts = {}
    crossed = []

    def spread(step):
        lefts[step] = Ring(links, "layer", lambda s: left.at[c, over(step), s])
        lefts[step].start()
        cross(step, 0)

    def cross(step, away):
        piece = left.at[c, over(step), lax.rem(x + away, 4)]
        crossed.append(links.copy(piece, piece, "col", 1))

    spread(0)
    y_up.wait_recv()
    spread(3)
    y_down.wait_recv()
    spread(1)
    y_up_pass.wait_recv()
    y_up_far = links.copy(left_pass.at[0], left.at[c, over(3), x, pl.ds(0, 64)], "y", 1)
    y_down_pass.wait_recv()
    y_down_far = links.copy(left_pass.at[1], left.at[c, over(1), x, pl.ds(64, 64)], "y", -1)
    rights[0].forward()
    rights[1].start()
    y_up_far.wait_recv()
    y_down_far.wait_recv()
    spread(2)
    for turn, step in enumerate((0, 3, 1, 2)):
        lefts[step].forward()
        cross(step, 3)
        cross(step, 1)
        if turn < 3:
            rights[turn + 1].forward()
            if turn < 2:
                rights[turn + 2].start()
    for step in (0, 3, 1, 2):
        lefts[step].finish()
        cross(step, 2)
    for made in crossed:
        made.wait_recv()

    def multiply(j, factor):
        def panel(i, carry):
            d = lax.rem(y + jnp.where(i == 0, 2, jnp.where(i == 1, 1, jnp.where(i == 2, 3, 0))), 4)
            total = jnp.zeros((512, WIDE), F32)
            for k in range(2):
                total += jnp.dot(
                    left[k, d].reshape(512, 1024),
                    factor[j, 2 * k : 2 * k + 2].reshape(1024, WIDE),
                    preferred_element_type=F32,
                )
            part[j, i] = total
            return carry

        lax.fori_loop(0, 4, panel, 0)

    class Sums:
        def __init__(self, j, stage):
            self.j, self.slot = j, stage * CHUNKS + j

        def send(self, n, value, step):
            sums_send[self.slot, n] = value.astype(BF16)
            return links.copy(sums_send.at[self.slot, n], sums_recv.at[self.slot, n], "y", step)

        def start(self):
            j = self.j
            self.made = [
                self.send(0, part[j, 0, 0:256], 1),
                self.send(1, part[j, 0, 256:512], -1),
                self.send(2, part[j, 1, 256:512], 1),
                self.send(3, part[j, 2, 0:256], -1),
            ]

        def combine(self):
            j = self.j
            self.made[0].wait_recv()
            self.made.append(self.send(4, part[j, 1, 0:256] + sums_recv[self.slot, 0].astype(F32), 1))
            self.made[1].wait_recv()
            self.made.append(self.send(5, part[j, 2, 256:512] + sums_recv[self.slot, 1].astype(F32), -1))

        def result(self):
            for n in (2, 3, 4, 5):
                self.made[n].wait_recv()
            halves = []
            for h, (a, b) in enumerate(((3, 4), (2, 5))):
                own = part[self.j, 3, h * 256 : (h + 1) * 256]
                halves.append(
                    own + sums_recv[self.slot, a].astype(F32) + sums_recv[self.slot, b].astype(F32)
                )
            return halves

    squares = [Sums(j, 0) for j in range(CHUNKS)]
    cubes = [Sums(j, 1) for j in range(CHUNKS)]
    gathers = [Ring(links, "z", lambda s, j=j: square.at[j, s]) for j in range(CHUNKS)]
    handed = []

    def first(j):
        rights[j].finish()
        multiply(j, right)
        squares[j].start()

    def squared(j):
        for h, value in enumerate(squares[j].result()):
            square[j, z, h * 256 : (h + 1) * 256] = value.astype(BF16)
        gathers[j].start()

    def second(j):
        gathers[j].finish()
        multiply(j, square)
        cubes[j].start()

    def purified(j):
        for h, value in enumerate(cubes[j].result()):
            for r in range(2):
                row = 2 * h + r
                for b in range(2):
                    lanes = slice(b * BS, (b + 1) * BS)
                    own = square[j, z, row * BS : (row + 1) * BS, lanes].astype(F32)
                    block = 3.0 * own - 2.0 * value[r * BS : (r + 1) * BS, lanes]
                    block = jnp.where(kept(row, x * 8 + j * 2 + b), block, jnp.zeros_like(block))
                    pure[j, row, b] = block.astype(BF16)
        where = x * 8 + j * 2
        for step in (1, 2, 3):
            to = lax.rem(x + step, 4)
            handed.append(links.copy(pure.at[j, to], held.at[pl.ds(where, 2)], "layer", step))
        for b in range(2):
            held[where + b] = pure[j, x, b]

    for made in requests:
        made.wait_recv()
    asked_rows[...] = asked_recv[:, 0, :]
    tables = [
        pltpu.make_async_copy(asked_rows, asked, in_sems.at[3]),
        pltpu.make_async_copy(spots, spot_of, in_sems.at[4]),
    ]
    for made in tables:
        made.start()
    first(0)
    first(1)
    for made in tables:
        made.wait()
    squares[0].combine()
    first(2)
    squares[1].combine()
    squared(0)
    first(3)
    squares[2].combine()
    squared(1)
    gathers[0].forward()
    squares[3].combine()
    second(0)
    squared(2)
    gathers[1].forward()
    cubes[0].combine()
    second(1)
    squared(3)
    gathers[2].forward()
    cubes[1].combine()
    purified(0)
    second(2)
    gathers[3].forward()
    cubes[2].combine()
    purified(1)
    second(3)
    cubes[3].combine()
    purified(2)
    purified(3)
    for made in handed:
        made.wait_recv()
    fetches = []
    for d in others:
        at = device(*d)
        to = holder_of(at)
        for k in range(2):
            picked[to, k] = held[asked[to, k]]
        fetches.append(links.to(picked.at[to], arrived.at[pl.ds(2 * me, 2)], at))
    for k in range(2):
        arrived[2 * me + k] = held[asked[me, k]]
    load_der.wait()
    for made in fetches:
        made.wait_recv()

    def contract(e, carry):
        block = arrived[spot_of[0, e]].astype(F32)
        for k in range(3):
            terms = block * der[e, k].astype(F32)
            contrib[k, e] = jnp.sum(terms.reshape(16, 8, BS), axis=0)
        return carry

    lax.fori_loop(0, 32, contract, 0)
    atoms = lax.broadcasted_iota(jnp.int32, (32, ATOM_DEV), 1)
    atom_hot = jnp.where(atoms_col[...] == atoms, 1.0, 0.0).astype(F32)
    for k in range(3):
        lanes = jnp.sum(contrib[k], axis=1)
        terms = lax.dot_general(
            jnp.ones((8, BS), F32), lanes, (((1,), (1,)), ((), ())),
            precision=lax.Precision.HIGHEST, preferred_element_type=F32,
        )
        summed = jnp.dot(terms, atom_hot, precision=lax.Precision.HIGHEST, preferred_element_type=F32)
        forces[k : k + 1, :] = -2.0 * summed[0:1, :]
    for made in links.started:
        made.wait_send()
    assert links.count == COPIES, links.count


def shards(density, pattern, holder, slot_index, atom_index, derivative):
    vmem = pl.BlockSpec(memory_space=pltpu.VMEM)
    hbm = pl.BlockSpec(memory_space=pl.ANY)
    return pl.pallas_call(
        purify_kernel,
        out_shape=jax.ShapeDtypeStruct((3, ATOM_DEV), F32),
        in_specs=[pl.BlockSpec(memory_space=pltpu.SMEM), hbm, vmem, vmem, vmem, vmem, hbm],
        out_specs=vmem,
        scratch_shapes=[
            pltpu.VMEM((BS, 4096), BF16),
            pltpu.VMEM((512, 1024), BF16),
            pltpu.VMEM((2, 4, 4, BS, 1024), BF16),
            pltpu.VMEM((4, BS, 1024), BF16),
            pltpu.VMEM((2, 64, 1024), BF16),
            pltpu.VMEM((CHUNKS, 4, 512, WIDE), BF16),
            pltpu.VMEM((CHUNKS, 4, 512, WIDE), BF16),
            pltpu.VMEM((CHUNKS, 4, 512, WIDE), F32),
            pltpu.VMEM((2 * CHUNKS, 6, 256, WIDE), BF16),
            pltpu.VMEM((2 * CHUNKS, 6, 256, WIDE), BF16),
            pltpu.VMEM((CHUNKS, 4, 2, BS, BS), BF16),
            pltpu.VMEM((32, BS, BS), BF16),
            pltpu.VMEM((32, 3, BS, BS), BF16),
            pltpu.VMEM((32, 8, BS), jnp.int32),
            pltpu.VMEM((32, 8, BS), jnp.int32),
            pltpu.VMEM((32, BS), jnp.int32),
            pltpu.VMEM((8, BS), jnp.int32),
            pltpu.SMEM((32, BS), jnp.int32),
            pltpu.SMEM((8, BS), jnp.int32),
            pltpu.VMEM((32, 2, BS, BS), BF16),
            pltpu.VMEM((64, BS, BS), BF16),
            pltpu.VMEM((3, 32, 8, BS), F32),
            pltpu.SemaphoreType.DMA((5,)),
            pltpu.SemaphoreType.DMA((COPIES,)),
            pltpu.SemaphoreType.DMA((COPIES,)),
        ],
        compiler_params=pltpu.CompilerParams(
            collective_id=0, has_side_effects=True, vmem_limit_bytes=60 << 20
        ),
    )(
        pattern, density, holder, holder.reshape(1, 32), slot_index.reshape(1, 32),
        atom_index.reshape(32, 1), derivative,
    )


def solution(mesh):
    split = Mesh(mesh.devices.reshape(4, 4, 4, 2), ("layer", "z", "y", "col"))
    every = ("layer", "z", "y", "col")
    return jax.shard_map(
        shards,
        mesh=split,
        in_specs=(
            P(("z", "y"), "col"),
            P(("z", "y"), "col"),
            P(every, None),
            P(every),
            P(every),
            P(every, None, None, None),
        ),
        out_specs=P(None, every),
        check_vma=False,
    )
```

```python
import jax
import jax.numpy as jnp
from jax import lax
from jax.experimental import pallas as pl
from jax.experimental.pallas import tpu as pltpu
from jax.sharding import Mesh, PartitionSpec as P

BS = 128
ATOM_DEV = 8
CHUNKS = 4
WIDE = 256
F32 = jnp.float32
BF16 = jnp.bfloat16
MESH = pl.DeviceIdType.MESH
COPIES = 182


class Links:
    def __init__(self, place, send_sems, recv_sems):
        self.place, self.send_sems, self.recv_sems = place, send_sems, recv_sems
        self.started = []
        self.count = 0

    def copy(self, src, dst, axis, step):
        length = 2 if axis == "col" else 4
        return self.to(src, dst, {axis: lax.rem(self.place[axis] + step + length, length)})

    def to(self, src, dst, device):
        number, self.count = self.count, self.count + 1
        made = pltpu.make_async_remote_copy(
            src_ref=src,
            dst_ref=dst,
            send_sem=self.send_sems.at[number],
            recv_sem=self.recv_sems.at[number],
            device_id=device,
            device_id_type=MESH,
        )
        made.start()
        self.started.append(made)
        return made


class Ring:
    def __init__(self, links, axis, slot):
        self.links, self.axis, self.slot = links, axis, slot
        self.own = links.place[axis]

    def start(self):
        mine = self.slot(self.own)
        self.up = self.links.copy(mine, mine, self.axis, 1)
        self.down = self.links.copy(mine, mine, self.axis, -1)

    def forward(self):
        half = self.slot(self.own).shape[0] // 2
        self.up.wait_recv()
        lower = self.slot(lax.rem(self.own + 3, 4)).at[pl.ds(0, half)]
        self.up_half = self.links.copy(lower, lower, self.axis, 1)
        self.down.wait_recv()
        upper = self.slot(lax.rem(self.own + 1, 4)).at[pl.ds(half, half)]
        self.down_half = self.links.copy(upper, upper, self.axis, -1)

    def finish(self):
        self.up_half.wait_recv()
        self.down_half.wait_recv()


def purify_kernel(
    pattern, density, targets_row, slots_row, atoms_row, derivative, forces,
    rows_in, cols_in, own_in, left, left_send, right, square, part, sums_send, sums_recv, pure, held,
    der, asked_send, asked_recv, asked_rows, spots, asked, spot_of, picked, arrived, contrib,
    in_sems, send_sems, recv_sems,
):
    x, z, y, c = (lax.axis_index(a) for a in ("layer", "z", "y", "col"))
    place = {"layer": x, "z": z, "y": y, "col": c}
    links = Links(place, send_sems, recv_sems)
    load_rows = pltpu.make_async_copy(
        density.at[pl.ds(pl.multiple_of(x * BS, BS), BS), :], rows_in, in_sems.at[0]
    )
    load_cols = pltpu.make_async_copy(
        density.at[:, pl.ds(pl.multiple_of(x * 1024, 1024), 1024)], cols_in, in_sems.at[1]
    )
    load_rows.start()
    load_cols.start()
    load_own = [
        pltpu.make_async_copy(
            density.at[:, pl.ds(pl.multiple_of(h * 2048 + y * 512, 512), 512)],
            own_in.at[h], in_sems.at[5 + h],
        )
        for h in range(2)
    ]
    for made in load_own:
        made.start()
    load_der = pltpu.make_async_copy(derivative, der, in_sems.at[2])
    load_der.start()
    barrier = pltpu.get_barrier_semaphore()
    others = [(dz, dy, dc) for dz in (2, 1, 3, 0) for dy in (2, 1, 3, 0) for dc in (0, 1)][:-2]
    others.append((0, 0, 1))

    def device(dz, dy, dc):
        return {"z": lax.rem(z + dz, 4), "y": lax.rem(y + dy, 4), "col": lax.rem(c + dc, 2)}

    def holder_of(at):
        return at["z"] * 8 + at["y"] * 2 + at["col"]

    me = z * 8 + y * 2 + c
    greeted = [device(*d) for d in others] + [{"layer": lax.rem(x + step, 4)} for step in (1, 2, 3)]
    for at in greeted:
        pl.semaphore_signal(barrier, inc=1, device_id=at, device_id_type=MESH)

    across = lax.broadcasted_iota(jnp.int32, (32, 32), 1)
    down = lax.broadcasted_iota(jnp.int32, (32, 32), 0)

    def column(row):
        return jnp.sum(jnp.where(down == across, row, 0), axis=1, keepdims=True)

    earlier = (column(targets_row[...]) == targets_row[...]) & (down < across)
    spot = 2 * targets_row[...] + jnp.sum(jnp.where(earlier, 1, 0), axis=0, keepdims=True)
    spots[...] = jnp.zeros_like(spots)
    spots[0:1, 0:32] = spot
    lane = lax.broadcasted_iota(jnp.int32, (32, BS), 1)
    table = jnp.zeros((32, BS), jnp.int32)
    for k in range(2):
        mine = jnp.where(spot == 2 * down + k, slots_row[...], 0)
        table = jnp.where(lane == k, jnp.sum(mine, axis=1, keepdims=True), table)
    asked_send[...] = jnp.broadcast_to(table[:, None, :], asked_send.shape)
    asked_recv[me] = asked_send[me]

    def kept(row_block, col_block):
        inside = pattern[row_block, col_block] == 1
        return inside | ((z * 4 + y) * 4 + row_block == c * 32 + col_block)

    load_rows.wait()
    for b in range(32):
        block = rows_in[:, b * BS : (b + 1) * BS]
        block = jnp.where(kept(x, b), block, jnp.zeros_like(block))
        lane = (b // 16) * 512 + (b % 4) * BS
        left_send[(b % 16) // 4, :, lane : lane + BS] = block
    pl.semaphore_wait(barrier, len(greeted))

    def over(step):
        return lax.rem(y + step, 4)

    brought = {
        step: links.copy(left_send.at[over(-step % 4)], left.at[c, y, x], "y", -step)
        for step in (3, 1, 2)
    }

    load_cols.wait()
    for b in range(8):
        for r in range(4):
            block = cols_in[r * BS : (r + 1) * BS, b * BS : (b + 1) * BS]
            block = jnp.where(kept(r, x * 8 + b), block, jnp.zeros_like(block))
            lane = (b % 2) * BS
            right[b // 2, z, r * BS : (r + 1) * BS, lane : lane + BS] = block
    requests = []
    for d in others:
        at = device(*d)
        requests.append(links.to(asked_send.at[holder_of(at)], asked_recv.at[me], at))
    rights = [Ring(links, "z", lambda s, j=j: right.at[j, s]) for j in range(CHUNKS)]
    rights[0].start()

    for made in load_own:
        made.wait()
    for h in range(2):
        for r in range(4):
            for w in range(4):
                block = own_in[h, r * BS : (r + 1) * BS, w * BS : (w + 1) * BS]
                block = jnp.where(kept(r, h * 16 + y * 4 + w), block, jnp.zeros_like(block))
                lane = h * 512 + w * BS
                left[c, y, r, :, lane : lane + BS] = block
    crossed = {0: [links.copy(left.at[c, y], left.at[c, y], "col", 1)], 1: [], 2: [], 3: []}
    lefts = {}

    def cross(step, away):
        piece = left.at[c, over(step), lax.rem(x + away, 4)]
        crossed[step].append(links.copy(piece, piece, "col", 1))

    def spread(step):
        brought[step].wait_recv()
        lefts[step] = Ring(links, "layer", lambda s: left.at[c, over(step), s])
        lefts[step].start()
        cross(step, 0)

    def relay(step):
        lefts[step].forward()
        cross(step, 3)
        cross(step, 1)

    def gathered(step):
        lefts[step].finish()
        cross(step, 2)

    def complete(*steps):
        for step in steps:
            for made in crossed[step]:
                made.wait_recv()

    def multiply(j, factor, panels):
        def panel(turn, carry):
            i = jnp.where(turn == 0, panels[0], panels[1])
            d = lax.rem(y + jnp.where(i == 0, 2, jnp.where(i == 1, 1, jnp.where(i == 2, 3, 0))), 4)
            total = jnp.zeros((512, WIDE), F32)
            for k in range(2):
                total += jnp.dot(
                    left[k, d].reshape(512, 1024),
                    factor[j, 2 * k : 2 * k + 2].reshape(1024, WIDE),
                    preferred_element_type=F32,
                )
            part[j, i] = total
            return carry

        lax.fori_loop(0, 2, panel, 0)

    class Sums:
        def __init__(self, j, stage):
            self.j, self.slot, self.made = j, stage * CHUNKS + j, {}

        def send(self, n, value, step):
            sums_send[self.slot, n] = value.astype(BF16)
            return links.copy(sums_send.at[self.slot, n], sums_recv.at[self.slot, n], "y", step)

        def far(self, factor):
            j = self.j
            multiply(j, factor, (0, 3))
            self.made[0] = self.send(0, part[j, 0, 0:256], 1)
            self.made[1] = self.send(1, part[j, 0, 256:512], -1)

        def near(self, factor):
            j = self.j
            multiply(j, factor, (1, 2))
            self.made[2] = self.send(2, part[j, 1, 256:512], 1)
            self.made[3] = self.send(3, part[j, 2, 0:256], -1)

        def combine(self):
            j = self.j
            self.made[0].wait_recv()
            self.made[4] = self.send(4, part[j, 1, 0:256] + sums_recv[self.slot, 0].astype(F32), 1)
            self.made[1].wait_recv()
            self.made[5] = self.send(5, part[j, 2, 256:512] + sums_recv[self.slot, 1].astype(F32), -1)

        def result(self):
            for n in (2, 3, 4, 5):
                self.made[n].wait_recv()
            halves = []
            for h, (a, b) in enumerate(((3, 4), (2, 5))):
                own = part[self.j, 3, h * 256 : (h + 1) * 256]
                halves.append(
                    own + sums_recv[self.slot, a].astype(F32) + sums_recv[self.slot, b].astype(F32)
                )
            return halves

    squares = [Sums(j, 0) for j in range(CHUNKS)]
    cubes = [Sums(j, 1) for j in range(CHUNKS)]
    gathers = [Ring(links, "z", lambda s, j=j: square.at[j, s]) for j in range(CHUNKS)]
    handed = []

    def squared(j):
        for h, value in enumerate(squares[j].result()):
            square[j, z, h * 256 : (h + 1) * 256] = value.astype(BF16)
        gathers[j].start()

    def second(j):
        gathers[j].finish()
        cubes[j].far(square)
        cubes[j].near(square)

    def purified(j):
        for h, value in enumerate(cubes[j].result()):
            for r in range(2):
                row = 2 * h + r
                for b in range(2):
                    lanes = slice(b * BS, (b + 1) * BS)
                    own = square[j, z, row * BS : (row + 1) * BS, lanes].astype(F32)
                    block = 3.0 * own - 2.0 * value[r * BS : (r + 1) * BS, lanes]
                    block = jnp.where(kept(row, x * 8 + j * 2 + b), block, jnp.zeros_like(block))
                    pure[j, row, b] = block.astype(BF16)
        where = x * 8 + j * 2
        for step in (1, 2, 3):
            to = lax.rem(x + step, 4)
            handed.append(links.copy(pure.at[j, to], held.at[pl.ds(where, 2)], "layer", step))
        for b in range(2):
            held[where + b] = pure[j, x, b]

    spread(3)
    spread(1)
    rights[0].forward()
    rights[1].start()
    spread(2)
    relay(3)
    relay(1)
    for made in requests:
        made.wait_recv()
    asked_rows[...] = asked_recv[:, 0, :]
    tables = [
        pltpu.make_async_copy(asked_rows, asked, in_sems.at[3]),
        pltpu.make_async_copy(spots, spot_of, in_sems.at[4]),
    ]
    for made in tables:
        made.start()
    gathered(3)
    gathered(1)
    rights[1].forward()
    rights[2].start()
    relay(2)
    for made in tables:
        made.wait()
    rights[0].finish()
    complete(0, 3, 1)
    squares[0].near(right)
    gathered(2)
    rights[1].finish()
    squares[1].near(right)
    rights[2].forward()
    rights[3].start()
    complete(2)
    squares[0].far(right)
    squares[1].far(right)
    squares[0].combine()
    rights[2].finish()
    squares[2].far(right)
    squares[2].near(right)
    squares[1].combine()
    squared(0)
    rights[3].forward()
    rights[3].finish()
    squares[3].far(right)
    squares[3].near(right)
    squares[2].combine()
    squared(1)
    gathers[0].forward()
    squares[3].combine()
    second(0)
    squared(2)
    gathers[1].forward()
    cubes[0].combine()
    second(1)
    squared(3)
    gathers[2].forward()
    cubes[1].combine()
    purified(0)
    second(2)
    gathers[3].forward()
    cubes[2].combine()
    purified(1)
    second(3)
    cubes[3].combine()
    purified(2)
    purified(3)
    for made in handed:
        made.wait_recv()
    fetches = []
    for d in others:
        at = device(*d)
        to = holder_of(at)
        for k in range(2):
            picked[to, k] = held[asked[to, k]]
        fetches.append(links.to(picked.at[to], arrived.at[pl.ds(2 * me, 2)], at))
    for k in range(2):
        arrived[2 * me + k] = held[asked[me, k]]
    load_der.wait()
    for made in fetches:
        made.wait_recv()

    def contract(e, carry):
        block = arrived[spot_of[0, e]].astype(F32)
        for k in range(3):
            terms = block * der[e, k].astype(F32)
            contrib[k, e] = jnp.sum(terms.reshape(16, 8, BS), axis=0)
        return carry

    lax.fori_loop(0, 32, contract, 0)
    atoms = lax.broadcasted_iota(jnp.int32, (32, ATOM_DEV), 1)
    atom_hot = jnp.where(column(atoms_row[...]) == atoms, 1.0, 0.0).astype(F32)
    for k in range(3):
        lanes = jnp.sum(contrib[k], axis=1)
        terms = lax.dot_general(
            jnp.ones((8, BS), F32), lanes, (((1,), (1,)), ((), ())),
            precision=lax.Precision.HIGHEST, preferred_element_type=F32,
        )
        summed = jnp.dot(terms, atom_hot, precision=lax.Precision.HIGHEST, preferred_element_type=F32)
        forces[k : k + 1, :] = -2.0 * summed[0:1, :]
    for made in links.started:
        made.wait_send()
    assert links.count == COPIES, links.count


def shards(density, pattern, holder, slot_index, atom_index, derivative):
    vmem = pl.BlockSpec(memory_space=pltpu.VMEM)
    hbm = pl.BlockSpec(memory_space=pl.ANY)
    return pl.pallas_call(
        purify_kernel,
        out_shape=jax.ShapeDtypeStruct((3, ATOM_DEV), F32),
        in_specs=[pl.BlockSpec(memory_space=pltpu.SMEM), hbm, vmem, vmem, vmem, hbm],
        out_specs=vmem,
        scratch_shapes=[
            pltpu.VMEM((BS, 4096), BF16),
            pltpu.VMEM((512, 1024), BF16),
            pltpu.VMEM((2, 512, 512), BF16),
            pltpu.VMEM((2, 4, 4, BS, 1024), BF16),
            pltpu.VMEM((4, BS, 1024), BF16),
            pltpu.VMEM((CHUNKS, 4, 512, WIDE), BF16),
            pltpu.VMEM((CHUNKS, 4, 512, WIDE), BF16),
            pltpu.VMEM((CHUNKS, 4, 512, WIDE), F32),
            pltpu.VMEM((2 * CHUNKS, 6, 256, WIDE), BF16),
            pltpu.VMEM((2 * CHUNKS, 6, 256, WIDE), BF16),
            pltpu.VMEM((CHUNKS, 4, 2, BS, BS), BF16),
            pltpu.VMEM((32, BS, BS), BF16),
            pltpu.VMEM((32, 3, BS, BS), BF16),
            pltpu.VMEM((32, 8, BS), jnp.int32),
            pltpu.VMEM((32, 8, BS), jnp.int32),
            pltpu.VMEM((32, BS), jnp.int32),
            pltpu.VMEM((8, BS), jnp.int32),
            pltpu.SMEM((32, BS), jnp.int32),
            pltpu.SMEM((8, BS), jnp.int32),
            pltpu.VMEM((32, 2, BS, BS), BF16),
            pltpu.VMEM((64, BS, BS), BF16),
            pltpu.VMEM((3, 32, 8, BS), F32),
            pltpu.SemaphoreType.DMA((7,)),
            pltpu.SemaphoreType.DMA((COPIES,)),
            pltpu.SemaphoreType.DMA((COPIES,)),
        ],
        compiler_params=pltpu.CompilerParams(
            collective_id=0, has_side_effects=True, vmem_limit_bytes=60 << 20
        ),
    )(
        pattern, density, holder.reshape(1, 32), slot_index.reshape(1, 32),
        atom_index.reshape(1, 32), derivative,
    )


def solution(mesh):
    split = Mesh(mesh.devices.reshape(4, 4, 4, 2), ("layer", "z", "y", "col"))
    every = ("layer", "z", "y", "col")
    return jax.shard_map(
        shards,
        mesh=split,
        in_specs=(
            P(("z", "y"), "col"),
            P(("z", "y"), "col"),
            P(every, None),
            P(every),
            P(every),
            P(every, None, None, None),
        ),
        out_specs=P(None, every),
        check_vma=False,
    )
```

```python
import jax
import jax.numpy as jnp
from jax import lax
from jax.experimental import pallas as pl
from jax.experimental.pallas import tpu as pltpu
from jax.sharding import Mesh, PartitionSpec as P

BS = 128
ATOM_DEV = 8
CHUNKS = 4
WIDE = 256
F32 = jnp.float32
BF16 = jnp.bfloat16
MESH = pl.DeviceIdType.MESH
COPIES = 175


class Links:
    def __init__(self, place, send_sems, recv_sems):
        self.place, self.send_sems, self.recv_sems = place, send_sems, recv_sems
        self.started = []
        self.count = 0

    def copy(self, src, dst, axis, step):
        length = 2 if axis == "col" else 4
        return self.to(src, dst, {axis: lax.rem(self.place[axis] + step + length, length)})

    def to(self, src, dst, device):
        number, self.count = self.count, self.count + 1
        made = pltpu.make_async_remote_copy(
            src_ref=src,
            dst_ref=dst,
            send_sem=self.send_sems.at[number],
            recv_sem=self.recv_sems.at[number],
            device_id=device,
            device_id_type=MESH,
        )
        made.start()
        self.started.append(made)
        return made


class Ring:
    def __init__(self, links, axis, slot):
        self.links, self.axis, self.slot = links, axis, slot
        self.own = links.place[axis]

    def start(self):
        mine = self.slot(self.own)
        self.up = self.links.copy(mine, mine, self.axis, 1)
        self.down = self.links.copy(mine, mine, self.axis, -1)

    def forward(self):
        half = self.slot(self.own).shape[0] // 2
        self.up.wait_recv()
        lower = self.slot(lax.rem(self.own + 3, 4)).at[pl.ds(0, half)]
        self.up_half = self.links.copy(lower, lower, self.axis, 1)
        self.down.wait_recv()
        upper = self.slot(lax.rem(self.own + 1, 4)).at[pl.ds(half, half)]
        self.down_half = self.links.copy(upper, upper, self.axis, -1)

    def finish(self):
        self.up_half.wait_recv()
        self.down_half.wait_recv()


def purify_kernel(
    pattern, density, targets_row, slots_row, atoms_row, derivative, forces,
    rows_in, cols_in, own_in, left, left_send, right, square, part, sums_send, sums_recv, pure, held,
    der, asked_send, asked_recv, asked_rows, spots, asked, spot_of, picked, arrived, contrib,
    in_sems, send_sems, recv_sems,
):
    x, z, y, c = (lax.axis_index(a) for a in ("layer", "z", "y", "col"))
    place = {"layer": x, "z": z, "y": y, "col": c}
    links = Links(place, send_sems, recv_sems)
    subs = [lax.rem(x + n, 4) for n in range(4)]
    load_rows = [
        pltpu.make_async_copy(
            density.at[pl.ds(pl.multiple_of(subs[n] * BS, BS), BS), :], rows_in.at[n], in_sems.at[n]
        )
        for n in range(2)
    ]
    load_cols = pltpu.make_async_copy(
        density.at[:, pl.ds(pl.multiple_of(x * 1024, 1024), 1024)], cols_in, in_sems.at[7]
    )
    for made in load_rows:
        made.start()
    load_cols.start()
    load_own = [
        pltpu.make_async_copy(
            density.at[:, pl.ds(pl.multiple_of(h * 2048 + y * 512, 512), 512)],
            own_in.at[h], in_sems.at[5 + h],
        )
        for h in range(2)
    ]
    for made in load_own:
        made.start()
    load_der = pltpu.make_async_copy(derivative, der, in_sems.at[2])
    load_der.start()
    barrier = pltpu.get_barrier_semaphore()
    hops = (0, 1, 2, 1)
    others = [(dz, dy, dc) for dz in range(4) for dy in range(4) for dc in range(2)][1:]
    others.sort(key=lambda d: -hops[d[0]] - hops[d[1]])

    def device(dz, dy, dc):
        return {"z": lax.rem(z + dz, 4), "y": lax.rem(y + dy, 4), "col": lax.rem(c + dc, 2)}

    def holder_of(at):
        return at["z"] * 8 + at["y"] * 2 + at["col"]

    me = z * 8 + y * 2 + c
    greeted = [device(*d) for d in others] + [{"layer": lax.rem(x + step, 4)} for step in (1, 2, 3)]
    for at in greeted:
        pl.semaphore_signal(barrier, inc=1, device_id=at, device_id_type=MESH)

    across = lax.broadcasted_iota(jnp.int32, (32, 32), 1)
    down = lax.broadcasted_iota(jnp.int32, (32, 32), 0)

    def column(row):
        return jnp.sum(jnp.where(down == across, row, 0), axis=1, keepdims=True)

    earlier = (column(targets_row[...]) == targets_row[...]) & (down < across)
    spot = 2 * targets_row[...] + jnp.sum(jnp.where(earlier, 1, 0), axis=0, keepdims=True)
    spots[...] = jnp.zeros_like(spots)
    spots[0:1, 0:32] = spot
    lane = lax.broadcasted_iota(jnp.int32, (32, BS), 1)
    table = jnp.zeros((32, BS), jnp.int32)
    for k in range(2):
        mine = jnp.where(spot == 2 * down + k, slots_row[...], 0)
        table = jnp.where(lane == k, jnp.sum(mine, axis=1, keepdims=True), table)
    asked_send[...] = jnp.broadcast_to(table[:, None, :], asked_send.shape)
    asked_recv[me] = asked_send[me]

    def kept(row_block, col_block):
        inside = pattern[row_block, col_block] == 1
        return inside | ((z * 4 + y) * 4 + row_block == c * 32 + col_block)

    def over(step):
        return lax.rem(y + step, 4)

    brought = {}

    def bring(step, n):
        brought[step, n] = links.copy(
            left_send.at[n, over(-step % 4)], left.at[c, y, subs[n]], "y", -step
        )

    for n in range(2):
        load_rows[n].wait()
        for b in range(32):
            block = rows_in[n, :, b * BS : (b + 1) * BS]
            block = jnp.where(kept(subs[n], b), block, jnp.zeros_like(block))
            lane = (b // 16) * 512 + (b % 4) * BS
            left_send[n, (b % 16) // 4, :, lane : lane + BS] = block
        if n == 0:
            pl.semaphore_wait(barrier, len(greeted))
        bring(3, n)
        bring(1, n)
    bring(2, 0)
    bring(2, 1)

    load_cols.wait()
    for b in range(8):
        for r in range(4):
            block = cols_in[r * BS : (r + 1) * BS, b * BS : (b + 1) * BS]
            block = jnp.where(kept(r, x * 8 + b), block, jnp.zeros_like(block))
            lane = (b % 2) * BS
            right[b // 2, z, r * BS : (r + 1) * BS, lane : lane + BS] = block
    requests = []
    for d in others:
        at = device(*d)
        requests.append(links.to(asked_send.at[holder_of(at)], asked_recv.at[me], at))
    rights = [
        [links.copy(right.at[j, z], right.at[j, z], "z", step) for step in (1, -1, 2)]
        for j in range(CHUNKS)
    ]

    for made in load_own:
        made.wait()
    for h in range(2):
        for r in range(4):
            for w in range(4):
                block = own_in[h, r * BS : (r + 1) * BS, w * BS : (w + 1) * BS]
                block = jnp.where(kept(r, h * 16 + y * 4 + w), block, jnp.zeros_like(block))
                lane = h * 512 + w * BS
                left[c, y, r, :, lane : lane + BS] = block
    crossed = {0: [links.copy(left.at[c, y], left.at[c, y], "col", 1)], 1: [], 2: [], 3: []}
    passed = {}

    def cross(step, away):
        piece = left.at[c, over(step), subs[away]]
        crossed[step].append(links.copy(piece, piece, "col", 1))

    def spread(step, n):
        brought[step, n].wait_recv()
        piece = left.at[c, over(step), subs[n]]
        passed[step, n] = links.copy(piece, piece, "layer", 1 - 2 * n)
        cross(step, n)

    def took(step, n):
        passed[step, n].wait_recv()
        cross(step, 3 - n)

    def complete(*steps):
        for step in steps:
            for made in crossed[step]:
                made.wait_recv()

    def multiply(j, factor, panels):
        def panel(turn, carry):
            i = jnp.where(turn == 0, panels[0], panels[1])
            d = lax.rem(y + jnp.where(i == 0, 2, jnp.where(i == 1, 1, jnp.where(i == 2, 3, 0))), 4)
            total = jnp.zeros((512, WIDE), F32)
            for k in range(2):
                total += jnp.dot(
                    left[k, d].reshape(512, 1024),
                    factor[j, 2 * k : 2 * k + 2].reshape(1024, WIDE),
                    preferred_element_type=F32,
                )
            part[j, i] = total
            return carry

        lax.fori_loop(0, 2, panel, 0)

    class Sums:
        def __init__(self, j, stage):
            self.j, self.slot, self.made = j, stage * CHUNKS + j, {}

        def send(self, n, value, step):
            sums_send[self.slot, n] = value.astype(BF16)
            return links.copy(sums_send.at[self.slot, n], sums_recv.at[self.slot, n], "y", step)

        def far(self, factor):
            j = self.j
            multiply(j, factor, (0, 3))
            self.made[0] = self.send(0, part[j, 0, 0:256], 1)
            self.made[1] = self.send(1, part[j, 0, 256:512], -1)

        def near(self, factor):
            j = self.j
            multiply(j, factor, (1, 2))
            self.made[2] = self.send(2, part[j, 1, 256:512], 1)
            self.made[3] = self.send(3, part[j, 2, 0:256], -1)

        def combine(self):
            j = self.j
            self.made[0].wait_recv()
            self.made[4] = self.send(4, part[j, 1, 0:256] + sums_recv[self.slot, 0].astype(F32), 1)
            self.made[1].wait_recv()
            self.made[5] = self.send(5, part[j, 2, 256:512] + sums_recv[self.slot, 1].astype(F32), -1)

        def result(self):
            for n in (2, 3, 4, 5):
                self.made[n].wait_recv()
            halves = []
            for h, (a, b) in enumerate(((3, 4), (2, 5))):
                own = part[self.j, 3, h * 256 : (h + 1) * 256]
                halves.append(
                    own + sums_recv[self.slot, a].astype(F32) + sums_recv[self.slot, b].astype(F32)
                )
            return halves

    squares = [Sums(j, 0) for j in range(CHUNKS)]
    cubes = [Sums(j, 1) for j in range(CHUNKS)]
    gathers = [Ring(links, "z", lambda s, j=j: square.at[j, s]) for j in range(CHUNKS)]
    handed = []

    def squared(j):
        for h, value in enumerate(squares[j].result()):
            square[j, z, h * 256 : (h + 1) * 256] = value.astype(BF16)
        gathers[j].start()

    def second(j):
        gathers[j].finish()
        cubes[j].far(square)
        cubes[j].near(square)

    def purified(j):
        for h, value in enumerate(cubes[j].result()):
            for r in range(2):
                row = 2 * h + r
                for b in range(2):
                    lanes = slice(b * BS, (b + 1) * BS)
                    own = square[j, z, row * BS : (row + 1) * BS, lanes].astype(F32)
                    block = 3.0 * own - 2.0 * value[r * BS : (r + 1) * BS, lanes]
                    block = jnp.where(kept(row, x * 8 + j * 2 + b), block, jnp.zeros_like(block))
                    pure[j, row, b] = block.astype(BF16)
        where = x * 8 + j * 2
        for step in (1, 2, 3):
            to = lax.rem(x + step, 4)
            handed.append(links.copy(pure.at[j, to], held.at[pl.ds(where, 2)], "layer", step))
        for b in range(2):
            held[where + b] = pure[j, x, b]

    def righted(j):
        for made in rights[j]:
            made.wait_recv()

    spread(3, 0)
    spread(1, 0)
    spread(3, 1)
    spread(1, 1)
    took(3, 0)
    spread(2, 0)
    took(3, 1)
    took(1, 0)
    spread(2, 1)
    for made in requests:
        made.wait_recv()
    asked_rows[...] = asked_recv[:, 0, :]
    tables = [
        pltpu.make_async_copy(asked_rows, asked, in_sems.at[3]),
        pltpu.make_async_copy(spots, spot_of, in_sems.at[4]),
    ]
    for made in tables:
        made.start()
    took(1, 1)
    took(2, 0)
    for made in tables:
        made.wait()
    righted(0)
    complete(0, 3, 1)
    squares[0].near(right)
    righted(1)
    squares[1].near(right)
    took(2, 1)
    complete(2)
    squares[0].far(right)
    squares[1].far(right)
    righted(2)
    squares[2].near(right)
    squares[0].combine()
    squares[2].far(right)
    squares[1].combine()
    squared(0)
    righted(3)
    squares[3].near(right)
    squares[2].combine()
    squares[3].far(right)
    squared(1)
    gathers[0].forward()
    squared(2)
    gathers[1].forward()
    squares[3].combine()
    second(0)
    squared(3)
    cubes[0].combine()
    gathers[2].forward()
    second(1)
    purified(0)
    cubes[1].combine()
    gathers[3].forward()
    second(2)
    purified(1)
    gathers[3].finish()
    cubes[3].far(square)
    cubes[2].combine()
    cubes[3].near(square)
    cubes[3].combine()
    purified(2)
    purified(3)
    for made in handed:
        made.wait_recv()
    fetches = []
    for d in others:
        at = device(*d)
        to = holder_of(at)
        for k in range(2):
            picked[to, k] = held[asked[to, k]]
        fetches.append(links.to(picked.at[to], arrived.at[pl.ds(2 * me, 2)], at))
    for k in range(2):
        arrived[2 * me + k] = held[asked[me, k]]
    load_der.wait()
    for made in fetches:
        made.wait_recv()

    def contract(e, carry):
        block = arrived[spot_of[0, e]].astype(F32)
        for k in range(3):
            terms = block * der[e, k].astype(F32)
            contrib[k, e] = jnp.sum(terms.reshape(16, 8, BS), axis=0)
        return carry

    lax.fori_loop(0, 32, contract, 0)
    atoms = lax.broadcasted_iota(jnp.int32, (32, ATOM_DEV), 1)
    atom_hot = jnp.where(column(atoms_row[...]) == atoms, 1.0, 0.0).astype(F32)
    for k in range(3):
        lanes = jnp.sum(contrib[k], axis=1)
        terms = lax.dot_general(
            jnp.ones((8, BS), F32), lanes, (((1,), (1,)), ((), ())),
            precision=lax.Precision.HIGHEST, preferred_element_type=F32,
        )
        summed = jnp.dot(terms, atom_hot, precision=lax.Precision.HIGHEST, preferred_element_type=F32)
        forces[k : k + 1, :] = -2.0 * summed[0:1, :]
    for made in links.started:
        made.wait_send()
    assert links.count == COPIES, links.count


def shards(density, pattern, holder, slot_index, atom_index, derivative):
    vmem = pl.BlockSpec(memory_space=pltpu.VMEM)
    hbm = pl.BlockSpec(memory_space=pl.ANY)
    return pl.pallas_call(
        purify_kernel,
        out_shape=jax.ShapeDtypeStruct((3, ATOM_DEV), F32),
        in_specs=[pl.BlockSpec(memory_space=pltpu.SMEM), hbm, vmem, vmem, vmem, hbm],
        out_specs=vmem,
        scratch_shapes=[
            pltpu.VMEM((2, BS, 4096), BF16),
            pltpu.VMEM((512, 1024), BF16),
            pltpu.VMEM((2, 512, 512), BF16),
            pltpu.VMEM((2, 4, 4, BS, 1024), BF16),
            pltpu.VMEM((2, 4, BS, 1024), BF16),
            pltpu.VMEM((CHUNKS, 4, 512, WIDE), BF16),
            pltpu.VMEM((CHUNKS, 4, 512, WIDE), BF16),
            pltpu.VMEM((CHUNKS, 4, 512, WIDE), F32),
            pltpu.VMEM((2 * CHUNKS, 6, 256, WIDE), BF16),
            pltpu.VMEM((2 * CHUNKS, 6, 256, WIDE), BF16),
            pltpu.VMEM((CHUNKS, 4, 2, BS, BS), BF16),
            pltpu.VMEM((32, BS, BS), BF16),
            pltpu.VMEM((32, 3, BS, BS), BF16),
            pltpu.VMEM((32, 8, BS), jnp.int32),
            pltpu.VMEM((32, 8, BS), jnp.int32),
            pltpu.VMEM((32, BS), jnp.int32),
            pltpu.VMEM((8, BS), jnp.int32),
            pltpu.SMEM((32, BS), jnp.int32),
            pltpu.SMEM((8, BS), jnp.int32),
            pltpu.VMEM((32, 2, BS, BS), BF16),
            pltpu.VMEM((64, BS, BS), BF16),
            pltpu.VMEM((3, 32, 8, BS), F32),
            pltpu.SemaphoreType.DMA((8,)),
            pltpu.SemaphoreType.DMA((COPIES,)),
            pltpu.SemaphoreType.DMA((COPIES,)),
        ],
        compiler_params=pltpu.CompilerParams(
            collective_id=0, has_side_effects=True, vmem_limit_bytes=60 << 20
        ),
    )(
        pattern, density, holder.reshape(1, 32), slot_index.reshape(1, 32),
        atom_index.reshape(1, 32), derivative,
    )


def solution(mesh):
    split = Mesh(mesh.devices.reshape(4, 4, 4, 2), ("layer", "z", "y", "col"))
    every = ("layer", "z", "y", "col")
    return jax.shard_map(
        shards,
        mesh=split,
        in_specs=(
            P(("z", "y"), "col"),
            P(("z", "y"), "col"),
            P(every, None),
            P(every),
            P(every),
            P(every, None, None, None),
        ),
        out_specs=P(None, every),
        check_vma=False,
    )
```

```python
import jax
import jax.numpy as jnp
from jax import lax
from jax.experimental import pallas as pl
from jax.experimental.pallas import tpu as pltpu
from jax.sharding import Mesh, PartitionSpec as P

BS = 128
ATOM_DEV = 8
CHUNKS = 4
WIDE = 256
F32 = jnp.float32
BF16 = jnp.bfloat16
MESH = pl.DeviceIdType.MESH
COPIES = 175


class Links:
    def __init__(self, place, send_sems, recv_sems):
        self.place, self.send_sems, self.recv_sems = place, send_sems, recv_sems
        self.started = []
        self.count = 0

    def copy(self, src, dst, axis, step):
        length = 2 if axis == "col" else 4
        return self.to(src, dst, {axis: lax.rem(self.place[axis] + step + length, length)})

    def to(self, src, dst, device):
        number, self.count = self.count, self.count + 1
        made = pltpu.make_async_remote_copy(
            src_ref=src,
            dst_ref=dst,
            send_sem=self.send_sems.at[number],
            recv_sem=self.recv_sems.at[number],
            device_id=device,
            device_id_type=MESH,
        )
        made.start()
        self.started.append(made)
        return made


class Ring:
    def __init__(self, links, axis, slot):
        self.links, self.axis, self.slot = links, axis, slot
        self.own = links.place[axis]

    def start(self):
        mine = self.slot(self.own)
        self.up = self.links.copy(mine, mine, self.axis, 1)
        self.down = self.links.copy(mine, mine, self.axis, -1)

    def forward(self):
        half = self.slot(self.own).shape[0] // 2
        self.up.wait_recv()
        lower = self.slot(lax.rem(self.own + 3, 4)).at[pl.ds(0, half)]
        self.up_half = self.links.copy(lower, lower, self.axis, 1)
        self.down.wait_recv()
        upper = self.slot(lax.rem(self.own + 1, 4)).at[pl.ds(half, half)]
        self.down_half = self.links.copy(upper, upper, self.axis, -1)

    def finish(self):
        self.up_half.wait_recv()
        self.down_half.wait_recv()


def purify_kernel(
    pattern, density, targets_row, slots_row, atoms_row, derivative, forces,
    rows_in, cols_in, own_in, left, left_send, right, square, part, sums_send, sums_recv, pure, held,
    der, asked_send, asked_recv, asked_rows, spots, asked, spot_of, picked, arrived, contrib,
    in_sems, send_sems, recv_sems,
):
    x, z, y, c = (lax.axis_index(a) for a in ("layer", "z", "y", "col"))
    place = {"layer": x, "z": z, "y": y, "col": c}
    links = Links(place, send_sems, recv_sems)
    subs = [lax.rem(x + n, 4) for n in range(4)]
    load_rows = [
        pltpu.make_async_copy(
            density.at[pl.ds(pl.multiple_of(subs[n] * BS, BS), BS), :], rows_in.at[n], in_sems.at[n]
        )
        for n in range(2)
    ]
    load_cols = pltpu.make_async_copy(
        density.at[:, pl.ds(pl.multiple_of(x * 1024, 1024), 1024)], cols_in, in_sems.at[7]
    )
    for made in load_rows:
        made.start()
    load_cols.start()
    load_own = [
        pltpu.make_async_copy(
            density.at[:, pl.ds(pl.multiple_of(h * 2048 + y * 512, 512), 512)],
            own_in.at[h], in_sems.at[5 + h],
        )
        for h in range(2)
    ]
    for made in load_own:
        made.start()
    load_der = pltpu.make_async_copy(derivative, der, in_sems.at[2])
    load_der.start()
    barrier = pltpu.get_barrier_semaphore()
    hops = (0, 1, 2, 1)
    others = [(dz, dy, dc) for dz in range(4) for dy in range(4) for dc in range(2)][1:]
    others.sort(key=lambda d: -hops[d[0]] - hops[d[1]])

    def device(dz, dy, dc):
        return {"z": lax.rem(z + dz, 4), "y": lax.rem(y + dy, 4), "col": lax.rem(c + dc, 2)}

    def holder_of(at):
        return at["z"] * 8 + at["y"] * 2 + at["col"]

    me = z * 8 + y * 2 + c
    greeted = [{"col": 1 - c}]
    for axis in ("y", "z", "layer"):
        greeted += [{axis: lax.rem(place[axis] + step, 4)} for step in (1, 2, 3)]
    for at in greeted:
        pl.semaphore_signal(barrier, inc=1, device_id=at, device_id_type=MESH)

    across = lax.broadcasted_iota(jnp.int32, (32, 32), 1)
    down = lax.broadcasted_iota(jnp.int32, (32, 32), 0)

    def column(row):
        return jnp.sum(jnp.where(down == across, row, 0), axis=1, keepdims=True)

    earlier = (column(targets_row[...]) == targets_row[...]) & (down < across)
    spot = 2 * targets_row[...] + jnp.sum(jnp.where(earlier, 1, 0), axis=0, keepdims=True)
    spots[...] = jnp.zeros_like(spots)
    spots[0:1, 0:32] = spot
    lane = lax.broadcasted_iota(jnp.int32, (32, BS), 1)
    table = jnp.zeros((32, BS), jnp.int32)
    for k in range(2):
        mine = jnp.where(spot == 2 * down + k, slots_row[...], 0)
        table = jnp.where(lane == k, jnp.sum(mine, axis=1, keepdims=True), table)
    asked_send[...] = jnp.broadcast_to(table[:, None, :], asked_send.shape)
    asked_recv[me] = asked_send[me]

    def kept(row_block, col_block):
        inside = pattern[row_block, col_block] == 1
        return inside | ((z * 4 + y) * 4 + row_block == c * 32 + col_block)

    def over(step):
        return lax.rem(y + step, 4)

    brought = {}

    def bring(step, n):
        brought[step, n] = links.copy(
            left_send.at[n, over(-step % 4)], left.at[c, y, subs[n]], "y", -step
        )

    for n in range(2):
        load_rows[n].wait()
        for b in range(32):
            block = rows_in[n, :, b * BS : (b + 1) * BS]
            block = jnp.where(kept(subs[n], b), block, jnp.zeros_like(block))
            lane = (b // 16) * 512 + (b % 4) * BS
            left_send[n, (b % 16) // 4, :, lane : lane + BS] = block
        if n == 0:
            pl.semaphore_wait(barrier, len(greeted))
        bring(3, n)
        bring(1, n)
    bring(2, 0)
    bring(2, 1)

    load_cols.wait()
    for b in range(8):
        for r in range(4):
            block = cols_in[r * BS : (r + 1) * BS, b * BS : (b + 1) * BS]
            block = jnp.where(kept(r, x * 8 + b), block, jnp.zeros_like(block))
            lane = (b % 2) * BS
            right[b // 2, z, r * BS : (r + 1) * BS, lane : lane + BS] = block
    rights = [
        [links.copy(right.at[j, z], right.at[j, z], "z", step) for step in (1, -1, 2)]
        for j in range(CHUNKS)
    ]

    for made in load_own:
        made.wait()
    for h in range(2):
        for r in range(4):
            for w in range(4):
                block = own_in[h, r * BS : (r + 1) * BS, w * BS : (w + 1) * BS]
                block = jnp.where(kept(r, h * 16 + y * 4 + w), block, jnp.zeros_like(block))
                lane = h * 512 + w * BS
                left[c, y, r, :, lane : lane + BS] = block
    crossed = {0: [links.copy(left.at[c, y], left.at[c, y], "col", 1)], 1: [], 2: [], 3: []}
    passed = {}

    def cross(step, away):
        piece = left.at[c, over(step), subs[away]]
        crossed[step].append(links.copy(piece, piece, "col", 1))

    def spread(step, n):
        brought[step, n].wait_recv()
        piece = left.at[c, over(step), subs[n]]
        passed[step, n] = links.copy(piece, piece, "layer", 1 - 2 * n)
        cross(step, n)

    def took(step, n):
        passed[step, n].wait_recv()
        cross(step, 3 - n)

    def complete(*steps):
        for step in steps:
            for made in crossed[step]:
                made.wait_recv()

    def multiply(j, factor, panels):
        def panel(turn, carry):
            i = jnp.where(turn == 0, panels[0], panels[1])
            d = lax.rem(y + jnp.where(i == 0, 2, jnp.where(i == 1, 1, jnp.where(i == 2, 3, 0))), 4)
            total = jnp.zeros((512, WIDE), F32)
            for k in range(2):
                total += jnp.dot(
                    left[k, d].reshape(512, 1024),
                    factor[j, 2 * k : 2 * k + 2].reshape(1024, WIDE),
                    preferred_element_type=F32,
                )
            part[j, i] = total
            return carry

        lax.fori_loop(0, 2, panel, 0)

    class Sums:
        def __init__(self, j, stage):
            self.j, self.slot, self.made = j, stage * CHUNKS + j, {}

        def send(self, n, value, step):
            sums_send[self.slot, n] = value.astype(BF16)
            return links.copy(sums_send.at[self.slot, n], sums_recv.at[self.slot, n], "y", step)

        def far(self, factor):
            j = self.j
            multiply(j, factor, (0, 3))
            self.made[0] = self.send(0, part[j, 0, 0:256], 1)
            self.made[1] = self.send(1, part[j, 0, 256:512], -1)

        def near(self, factor):
            j = self.j
            multiply(j, factor, (1, 2))
            self.made[2] = self.send(2, part[j, 1, 256:512], 1)
            self.made[3] = self.send(3, part[j, 2, 0:256], -1)

        def combine(self):
            j = self.j
            self.made[0].wait_recv()
            self.made[4] = self.send(4, part[j, 1, 0:256] + sums_recv[self.slot, 0].astype(F32), 1)
            self.made[1].wait_recv()
            self.made[5] = self.send(5, part[j, 2, 256:512] + sums_recv[self.slot, 1].astype(F32), -1)

        def result(self):
            for n in (2, 3, 4, 5):
                self.made[n].wait_recv()
            halves = []
            for h, (a, b) in enumerate(((3, 4), (2, 5))):
                own = part[self.j, 3, h * 256 : (h + 1) * 256]
                halves.append(
                    own + sums_recv[self.slot, a].astype(F32) + sums_recv[self.slot, b].astype(F32)
                )
            return halves

    squares = [Sums(j, 0) for j in range(CHUNKS)]
    cubes = [Sums(j, 1) for j in range(CHUNKS)]
    gathers = [Ring(links, "z", lambda s, j=j: square.at[j, s]) for j in range(CHUNKS)]
    handed = []

    def squared(j):
        for h, value in enumerate(squares[j].result()):
            square[j, z, h * 256 : (h + 1) * 256] = value.astype(BF16)
        gathers[j].start()

    def second(j):
        gathers[j].finish()
        cubes[j].far(square)
        cubes[j].near(square)

    def purified(j):
        for h, value in enumerate(cubes[j].result()):
            for r in range(2):
                row = 2 * h + r
                for b in range(2):
                    lanes = slice(b * BS, (b + 1) * BS)
                    own = square[j, z, row * BS : (row + 1) * BS, lanes].astype(F32)
                    block = 3.0 * own - 2.0 * value[r * BS : (r + 1) * BS, lanes]
                    block = jnp.where(kept(row, x * 8 + j * 2 + b), block, jnp.zeros_like(block))
                    pure[j, row, b] = block.astype(BF16)
        where = x * 8 + j * 2
        for step in (1, 2, 3):
            to = lax.rem(x + step, 4)
            handed.append(links.copy(pure.at[j, to], held.at[pl.ds(where, 2)], "layer", step))
        for b in range(2):
            held[where + b] = pure[j, x, b]

    def righted(j):
        for made in rights[j]:
            made.wait_recv()

    spread(3, 0)
    spread(1, 0)
    spread(3, 1)
    spread(1, 1)
    took(3, 0)
    spread(2, 0)
    took(3, 1)
    took(1, 0)
    spread(2, 1)
    took(1, 1)
    took(2, 0)
    righted(0)
    complete(0, 3, 1)
    squares[0].near(right)
    righted(1)
    squares[1].near(right)
    took(2, 1)
    complete(2)
    squares[0].far(right)
    squares[1].far(right)
    righted(2)
    squares[2].near(right)
    squares[0].combine()
    squares[2].far(right)
    squares[1].combine()
    squared(0)
    requests = []
    for d in others:
        at = device(*d)
        requests.append(links.to(asked_send.at[holder_of(at)], asked_recv.at[me], at))
    righted(3)
    squares[3].near(right)
    squares[2].combine()
    squares[3].far(right)
    squared(1)
    gathers[0].forward()
    squared(2)
    gathers[1].forward()
    squares[3].combine()
    second(0)
    squared(3)
    cubes[0].combine()
    gathers[2].forward()
    second(1)
    for made in requests:
        made.wait_recv()
    asked_rows[...] = asked_recv[:, 0, :]
    tables = [
        pltpu.make_async_copy(asked_rows, asked, in_sems.at[3]),
        pltpu.make_async_copy(spots, spot_of, in_sems.at[4]),
    ]
    for made in tables:
        made.start()
    purified(0)
    cubes[1].combine()
    gathers[3].forward()
    second(2)
    purified(1)
    gathers[3].finish()
    cubes[3].far(square)
    cubes[2].combine()
    cubes[3].near(square)
    cubes[3].combine()
    purified(2)
    purified(3)
    for made in handed:
        made.wait_recv()
    for made in tables:
        made.wait()
    fetches = []
    for d in others:
        at = device(*d)
        to = holder_of(at)
        for k in range(2):
            picked[to, k] = held[asked[to, k]]
        fetches.append(links.to(picked.at[to], arrived.at[pl.ds(2 * me, 2)], at))
    for k in range(2):
        arrived[2 * me + k] = held[asked[me, k]]
    load_der.wait()
    for made in fetches:
        made.wait_recv()

    def contract(e, carry):
        block = arrived[spot_of[0, e]].astype(F32)
        for k in range(3):
            terms = block * der[e, k].astype(F32)
            contrib[k, e] = jnp.sum(terms.reshape(16, 8, BS), axis=0)
        return carry

    lax.fori_loop(0, 32, contract, 0)
    atoms = lax.broadcasted_iota(jnp.int32, (32, ATOM_DEV), 1)
    atom_hot = jnp.where(column(atoms_row[...]) == atoms, 1.0, 0.0).astype(F32)
    for k in range(3):
        lanes = jnp.sum(contrib[k], axis=1)
        terms = lax.dot_general(
            jnp.ones((8, BS), F32), lanes, (((1,), (1,)), ((), ())),
            precision=lax.Precision.HIGHEST, preferred_element_type=F32,
        )
        summed = jnp.dot(terms, atom_hot, precision=lax.Precision.HIGHEST, preferred_element_type=F32)
        forces[k : k + 1, :] = -2.0 * summed[0:1, :]
    for made in links.started:
        made.wait_send()
    assert links.count == COPIES, links.count


def shards(density, pattern, holder, slot_index, atom_index, derivative):
    vmem = pl.BlockSpec(memory_space=pltpu.VMEM)
    hbm = pl.BlockSpec(memory_space=pl.ANY)
    return pl.pallas_call(
        purify_kernel,
        out_shape=jax.ShapeDtypeStruct((3, ATOM_DEV), F32),
        in_specs=[pl.BlockSpec(memory_space=pltpu.SMEM), hbm, vmem, vmem, vmem, hbm],
        out_specs=vmem,
        scratch_shapes=[
            pltpu.VMEM((2, BS, 4096), BF16),
            pltpu.VMEM((512, 1024), BF16),
            pltpu.VMEM((2, 512, 512), BF16),
            pltpu.VMEM((2, 4, 4, BS, 1024), BF16),
            pltpu.VMEM((2, 4, BS, 1024), BF16),
            pltpu.VMEM((CHUNKS, 4, 512, WIDE), BF16),
            pltpu.VMEM((CHUNKS, 4, 512, WIDE), BF16),
            pltpu.VMEM((CHUNKS, 4, 512, WIDE), F32),
            pltpu.VMEM((2 * CHUNKS, 6, 256, WIDE), BF16),
            pltpu.VMEM((2 * CHUNKS, 6, 256, WIDE), BF16),
            pltpu.VMEM((CHUNKS, 4, 2, BS, BS), BF16),
            pltpu.VMEM((32, BS, BS), BF16),
            pltpu.VMEM((32, 3, BS, BS), BF16),
            pltpu.VMEM((32, 8, BS), jnp.int32),
            pltpu.VMEM((32, 8, BS), jnp.int32),
            pltpu.VMEM((32, BS), jnp.int32),
            pltpu.VMEM((8, BS), jnp.int32),
            pltpu.SMEM((32, BS), jnp.int32),
            pltpu.SMEM((8, BS), jnp.int32),
            pltpu.VMEM((32, 2, BS, BS), BF16),
            pltpu.VMEM((64, BS, BS), BF16),
            pltpu.VMEM((3, 32, 8, BS), F32),
            pltpu.SemaphoreType.DMA((8,)),
            pltpu.SemaphoreType.DMA((COPIES,)),
            pltpu.SemaphoreType.DMA((COPIES,)),
        ],
        compiler_params=pltpu.CompilerParams(
            collective_id=0, has_side_effects=True, vmem_limit_bytes=60 << 20
        ),
    )(
        pattern, density, holder.reshape(1, 32), slot_index.reshape(1, 32),
        atom_index.reshape(1, 32), derivative,
    )


def solution(mesh):
    split = Mesh(mesh.devices.reshape(4, 4, 4, 2), ("layer", "z", "y", "col"))
    every = ("layer", "z", "y", "col")
    return jax.shard_map(
        shards,
        mesh=split,
        in_specs=(
            P(("z", "y"), "col"),
            P(("z", "y"), "col"),
            P(every, None),
            P(every),
            P(every),
            P(every, None, None, None),
        ),
        out_specs=P(None, every),
        check_vma=False,
    )
```

```python
import jax
import jax.numpy as jnp
from jax import lax
from jax.experimental import pallas as pl
from jax.experimental.pallas import tpu as pltpu
from jax.sharding import Mesh, PartitionSpec as P

BS = 128
ATOM_DEV = 8
CHUNKS = 4
WIDE = 256
F32 = jnp.float32
BF16 = jnp.bfloat16
MESH = pl.DeviceIdType.MESH
COPIES = 242


class Links:
    def __init__(self, place, send_sems, recv_sems):
        self.place, self.send_sems, self.recv_sems = place, send_sems, recv_sems
        self.started = []
        self.count = 0

    def copy(self, src, dst, axis, step):
        length = 2 if axis == "col" else 4
        return self.to(src, dst, {axis: lax.rem(self.place[axis] + step + length, length)})

    def to(self, src, dst, device):
        number, self.count = self.count, self.count + 1
        made = pltpu.make_async_remote_copy(
            src_ref=src,
            dst_ref=dst,
            send_sem=self.send_sems.at[number],
            recv_sem=self.recv_sems.at[number],
            device_id=device,
            device_id_type=MESH,
        )
        made.start()
        self.started.append(made)
        return made


class Ring:
    def __init__(self, links, axis, slot):
        self.links, self.axis, self.slot = links, axis, slot
        self.own = links.place[axis]

    def start(self):
        mine = self.slot(self.own)
        self.up = self.links.copy(mine, mine, self.axis, 1)
        self.down = self.links.copy(mine, mine, self.axis, -1)

    def forward(self):
        half = self.slot(self.own).shape[0] // 2
        self.up.wait_recv()
        lower = self.slot(lax.rem(self.own + 3, 4)).at[pl.ds(0, half)]
        self.up_half = self.links.copy(lower, lower, self.axis, 1)
        self.down.wait_recv()
        upper = self.slot(lax.rem(self.own + 1, 4)).at[pl.ds(half, half)]
        self.down_half = self.links.copy(upper, upper, self.axis, -1)

    def finish(self):
        self.up_half.wait_recv()
        self.down_half.wait_recv()


def purify_kernel(
    pattern, density, targets_row, slots_row, atoms_row, derivative, forces,
    rows_in, cols_in, own_in, left, left_send, right, square, part, sums_send, sums_recv, cube_send, cube_recv, pure, held_low, held_high,
    der, asked_send, asked_recv, asked_rows, spots, asked, spot_of, picked, arrived_low, arrived_high, contrib,
    in_sems, send_sems, recv_sems,
):
    held, arrived = (held_low, held_high), (arrived_low, arrived_high)
    x, z, y, c = (lax.axis_index(a) for a in ("layer", "z", "y", "col"))
    place = {"layer": x, "z": z, "y": y, "col": c}
    links = Links(place, send_sems, recv_sems)
    subs = [lax.rem(x + n, 4) for n in range(4)]
    load_rows = [
        pltpu.make_async_copy(
            density.at[pl.ds(pl.multiple_of(subs[n] * BS, BS), BS), :], rows_in.at[n], in_sems.at[n]
        )
        for n in range(2)
    ]
    load_cols = pltpu.make_async_copy(
        density.at[:, pl.ds(pl.multiple_of(x * 1024, 1024), 1024)], cols_in, in_sems.at[7]
    )
    for made in load_rows:
        made.start()
    load_cols.start()
    load_own = [
        pltpu.make_async_copy(
            density.at[:, pl.ds(pl.multiple_of(h * 2048 + y * 512, 512), 512)],
            own_in.at[h], in_sems.at[5 + h],
        )
        for h in range(2)
    ]
    for made in load_own:
        made.start()
    load_der = pltpu.make_async_copy(derivative, der, in_sems.at[2])
    load_der.start()
    barrier = pltpu.get_barrier_semaphore()
    hops = (0, 1, 2, 1)
    others = [(dz, dy, dc) for dz in range(4) for dy in range(4) for dc in range(2)][1:]
    others.sort(key=lambda d: -hops[d[0]] - hops[d[1]])

    def device(dz, dy, dc):
        return {"z": lax.rem(z + dz, 4), "y": lax.rem(y + dy, 4), "col": lax.rem(c + dc, 2)}

    def holder_of(at):
        return at["z"] * 8 + at["y"] * 2 + at["col"]

    me = z * 8 + y * 2 + c
    greeted = [device(*d) for d in others] + [{"layer": lax.rem(x + step, 4)} for step in (1, 2, 3)]
    for at in greeted:
        pl.semaphore_signal(barrier, inc=1, device_id=at, device_id_type=MESH)

    across = lax.broadcasted_iota(jnp.int32, (32, 32), 1)
    down = lax.broadcasted_iota(jnp.int32, (32, 32), 0)

    def column(row):
        return jnp.sum(jnp.where(down == across, row, 0), axis=1, keepdims=True)

    earlier = (column(targets_row[...]) == targets_row[...]) & (down < across)
    spot = 2 * targets_row[...] + jnp.sum(jnp.where(earlier, 1, 0), axis=0, keepdims=True)
    spots[...] = jnp.zeros_like(spots)
    spots[0:1, 0:32] = spot
    lane = lax.broadcasted_iota(jnp.int32, (32, BS), 1)
    table = jnp.zeros((32, BS), jnp.int32)
    for k in range(2):
        mine = jnp.where(spot == 2 * down + k, slots_row[...], 0)
        table = jnp.where(lane == k, jnp.sum(mine, axis=1, keepdims=True), table)
    asked_send[...] = jnp.broadcast_to(table[:, None, :], asked_send.shape)
    asked_recv[me] = asked_send[me]

    def kept(row_block, col_block):
        inside = pattern[row_block, col_block] == 1
        return inside | ((z * 4 + y) * 4 + row_block == c * 32 + col_block)

    def over(step):
        return lax.rem(y + step, 4)

    brought = {}

    def bring(step, n):
        brought[step, n] = links.copy(
            left_send.at[n, over(-step % 4)], left.at[c, y, subs[n]], "y", -step
        )

    for n in range(2):
        load_rows[n].wait()
        for b in range(32):
            block = rows_in[n, :, b * BS : (b + 1) * BS]
            block = jnp.where(kept(subs[n], b), block, jnp.zeros_like(block))
            lane = (b // 16) * 512 + (b % 4) * BS
            left_send[n, (b % 16) // 4, :, lane : lane + BS] = block
        if n == 0:
            pl.semaphore_wait(barrier, len(greeted))
        bring(3, n)
        bring(1, n)
    bring(2, 0)
    bring(2, 1)

    load_cols.wait()
    for b in range(8):
        for r in range(4):
            block = cols_in[r * BS : (r + 1) * BS, b * BS : (b + 1) * BS]
            block = jnp.where(kept(r, x * 8 + b), block, jnp.zeros_like(block))
            lane = (b % 2) * BS
            right[b // 2, z, r * BS : (r + 1) * BS, lane : lane + BS] = block
    requests = []
    for d in others:
        at = device(*d)
        requests.append(links.to(asked_send.at[holder_of(at)], asked_recv.at[me], at))
    rights = [
        [links.copy(right.at[j, z], right.at[j, z], "z", step) for step in (1, -1, 2)]
        for j in range(CHUNKS)
    ]

    for made in load_own:
        made.wait()
    for h in range(2):
        for r in range(4):
            for w in range(4):
                block = own_in[h, r * BS : (r + 1) * BS, w * BS : (w + 1) * BS]
                block = jnp.where(kept(r, h * 16 + y * 4 + w), block, jnp.zeros_like(block))
                lane = h * 512 + w * BS
                left[c, y, r, :, lane : lane + BS] = block
    crossed = {0: [links.copy(left.at[c, y], left.at[c, y], "col", 1)], 1: [], 2: [], 3: []}
    passed = {}

    def cross(step, away):
        piece = left.at[c, over(step), subs[away]]
        crossed[step].append(links.copy(piece, piece, "col", 1))

    def spread(step, n):
        brought[step, n].wait_recv()
        piece = left.at[c, over(step), subs[n]]
        passed[step, n] = links.copy(piece, piece, "layer", 1 - 2 * n)
        cross(step, n)

    def took(step, n):
        passed[step, n].wait_recv()
        cross(step, 3 - n)

    def complete(*steps):
        for step in steps:
            for made in crossed[step]:
                made.wait_recv()

    def multiply(j, factor, panels, half):
        height = 512 if half is None else 256
        base = 256 * (half or 0)

        def panel(turn, carry):
            i = jnp.where(turn == 0, panels[0], panels[1])
            d = lax.rem(y + jnp.where(i == 0, 2, jnp.where(i == 1, 1, jnp.where(i == 2, 3, 0))), 4)
            total = jnp.zeros((height, WIDE), F32)
            for k in range(2):
                if half is None:
                    rows = left[k, d]
                else:
                    rows = left[k, d, :, 64 * half : 64 * half + 64, :]
                total += jnp.dot(
                    rows.reshape(height, 1024),
                    factor[j, 2 * k : 2 * k + 2].reshape(1024, WIDE),
                    preferred_element_type=F32,
                )
            part[j, i, base : base + height] = total
            return carry

        lax.fori_loop(0, 2, panel, 0)

    class Sums:
        def __init__(self, j, half, factor, sent, received):
            self.j, self.half, self.factor = j, half, factor
            self.sent, self.received, self.made = sent, received, {}
            self.low = 256 * (half or 0)
            self.size = 256 if half is None else 128

        def own(self, i, upper):
            start = self.low + self.size * upper
            return part[self.j, i, start : start + self.size]

        def send(self, n, value, step):
            self.sent[n] = value.astype(BF16)
            self.made[n] = links.copy(self.sent.at[n], self.received.at[n], "y", step)

        def far(self):
            multiply(self.j, self.factor, (0, 3), self.half)
            self.send(0, self.own(0, 0), 1)
            self.send(1, self.own(0, 1), -1)

        def near(self):
            multiply(self.j, self.factor, (1, 2), self.half)
            self.send(2, self.own(1, 1), 1)
            self.send(3, self.own(2, 0), -1)

        def combine(self):
            self.made[0].wait_recv()
            self.send(4, self.own(1, 0) + self.received[0].astype(F32), 1)
            self.made[1].wait_recv()
            self.send(5, self.own(2, 1) + self.received[1].astype(F32), -1)

        def result(self):
            for n in (2, 3, 4, 5):
                self.made[n].wait_recv()
            return [
                self.own(3, h) + self.received[a].astype(F32) + self.received[b].astype(F32)
                for h, (a, b) in enumerate(((3, 4), (2, 5)))
            ]

    squares = [Sums(j, None, right, sums_send.at[j], sums_recv.at[j]) for j in range(CHUNKS)]
    cubes = [
        [
            Sums(j, half, square, cube_send.at[half, j], cube_recv.at[half, j])
            for j in range(CHUNKS)
        ]
        for half in range(2)
    ]
    gathers = [Ring(links, "z", lambda s, j=j: square.at[j, s]) for j in range(CHUNKS)]
    handed = [[], []]

    def squared(j):
        for h, value in enumerate(squares[j].result()):
            square[j, z, h * 256 : (h + 1) * 256] = value.astype(BF16)
        gathers[j].start()

    gone = set()

    def second(half, j):
        if j not in gone:
            gathers[j].finish()
            gone.add(j)
        cubes[half][j].far()
        cubes[half][j].near()

    def purified(half, j):
        for h, value in enumerate(cubes[half][j].result()):
            for r in range(2):
                row = 2 * h + r
                start = row * BS + 64 * half
                for b in range(2):
                    lanes = slice(b * BS, (b + 1) * BS)
                    own = square[j, z, start : start + 64, lanes].astype(F32)
                    block = 3.0 * own - 2.0 * value[64 * r : 64 * r + 64, lanes]
                    block = jnp.where(kept(row, x * 8 + j * 2 + b), block, jnp.zeros_like(block))
                    pure[half, j, row, b] = block.astype(BF16)
        where = x * 8 + j * 2
        for step in (1, 2, 3):
            to = lax.rem(x + step, 4)
            handed[half].append(
                links.copy(pure.at[half, j, to], held[half].at[pl.ds(where, 2)], "layer", step)
            )
        for b in range(2):
            held[half][where + b] = pure[half, j, x, b]

    fetches = [[], []]

    def fetch(half):
        for made in handed[half]:
            made.wait_recv()
        for d in others:
            at = device(*d)
            to = holder_of(at)
            for k in range(2):
                picked[half, to, k] = held[half][asked[to, k]]
            fetches[half].append(
                links.to(picked.at[half, to], arrived[half].at[pl.ds(2 * me, 2)], at)
            )
        for k in range(2):
            arrived[half][2 * me + k] = held[half][asked[me, k]]

    def contract(half):
        for made in fetches[half]:
            made.wait_recv()

        def entry(e, carry):
            block = arrived[half][spot_of[0, e]].astype(F32)
            for k in range(3):
                terms = block * der[e, k, 64 * half : 64 * half + 64, :].astype(F32)
                total = jnp.sum(terms.reshape(8, 8, BS), axis=0)
                contrib[k, e] = total if half == 0 else contrib[k, e] + total
            return carry

        lax.fori_loop(0, 32, entry, 0)

    def righted(j):
        for made in rights[j]:
            made.wait_recv()

    spread(3, 0)
    spread(1, 0)
    spread(3, 1)
    spread(1, 1)
    took(3, 0)
    spread(2, 0)
    took(3, 1)
    took(1, 0)
    spread(2, 1)
    for made in requests:
        made.wait_recv()
    asked_rows[...] = asked_recv[:, 0, :]
    tables = [
        pltpu.make_async_copy(asked_rows, asked, in_sems.at[3]),
        pltpu.make_async_copy(spots, spot_of, in_sems.at[4]),
    ]
    for made in tables:
        made.start()
    took(1, 1)
    took(2, 0)
    for made in tables:
        made.wait()
    complete(0, 3, 1)
    for j in (0, 1):
        righted(j)
        squares[j].near()
    took(2, 1)
    complete(2)
    squares[0].far()
    squares[1].far()
    squares[0].combine()
    squares[1].combine()
    righted(2)
    squares[2].near()
    squares[2].far()
    squared(0)
    squared(1)
    righted(3)
    squares[3].near()
    squares[3].far()
    squares[2].combine()
    gathers[0].forward()
    squares[3].combine()
    gathers[1].forward()
    squared(2)
    second(0, 0)
    cubes[0][0].combine()
    second(1, 0)
    squared(3)
    second(0, 1)
    cubes[1][0].combine()
    gathers[2].forward()
    second(1, 1)
    cubes[0][1].combine()
    purified(0, 0)
    purified(1, 0)
    gathers[3].forward()
    cubes[1][1].combine()
    second(0, 2)
    purified(0, 1)
    second(0, 3)
    purified(1, 1)
    cubes[0][2].combine()
    cubes[0][3].combine()
    second(1, 2)
    second(1, 3)
    purified(0, 2)
    purified(0, 3)
    cubes[1][2].combine()
    cubes[1][3].combine()
    fetch(0)
    purified(1, 2)
    purified(1, 3)
    load_der.wait()
    fetch(1)
    contract(0)
    contract(1)
    atoms = lax.broadcasted_iota(jnp.int32, (32, ATOM_DEV), 1)
    atom_hot = jnp.where(column(atoms_row[...]) == atoms, 1.0, 0.0).astype(F32)
    for k in range(3):
        lanes = jnp.sum(contrib[k], axis=1)
        terms = lax.dot_general(
            jnp.ones((8, BS), F32), lanes, (((1,), (1,)), ((), ())),
            precision=lax.Precision.HIGHEST, preferred_element_type=F32,
        )
        summed = jnp.dot(terms, atom_hot, precision=lax.Precision.HIGHEST, preferred_element_type=F32)
        forces[k : k + 1, :] = -2.0 * summed[0:1, :]
    for made in links.started:
        made.wait_send()
    assert links.count == COPIES, links.count


def shards(density, pattern, holder, slot_index, atom_index, derivative):
    vmem = pl.BlockSpec(memory_space=pltpu.VMEM)
    hbm = pl.BlockSpec(memory_space=pl.ANY)
    return pl.pallas_call(
        purify_kernel,
        out_shape=jax.ShapeDtypeStruct((3, ATOM_DEV), F32),
        in_specs=[pl.BlockSpec(memory_space=pltpu.SMEM), hbm, vmem, vmem, vmem, hbm],
        out_specs=vmem,
        scratch_shapes=[
            pltpu.VMEM((2, BS, 4096), BF16),
            pltpu.VMEM((512, 1024), BF16),
            pltpu.VMEM((2, 512, 512), BF16),
            pltpu.VMEM((2, 4, 4, BS, 1024), BF16),
            pltpu.VMEM((2, 4, BS, 1024), BF16),
            pltpu.VMEM((CHUNKS, 4, 512, WIDE), BF16),
            pltpu.VMEM((CHUNKS, 4, 512, WIDE), BF16),
            pltpu.VMEM((CHUNKS, 4, 512, WIDE), F32),
            pltpu.VMEM((CHUNKS, 6, 256, WIDE), BF16),
            pltpu.VMEM((CHUNKS, 6, 256, WIDE), BF16),
            pltpu.VMEM((2, CHUNKS, 6, BS, WIDE), BF16),
            pltpu.VMEM((2, CHUNKS, 6, BS, WIDE), BF16),
            pltpu.VMEM((2, CHUNKS, 4, 2, 64, BS), BF16),
            pltpu.VMEM((32, 64, BS), BF16),
            pltpu.VMEM((32, 64, BS), BF16),
            pltpu.VMEM((32, 3, BS, BS), BF16),
            pltpu.VMEM((32, 8, BS), jnp.int32),
            pltpu.VMEM((32, 8, BS), jnp.int32),
            pltpu.VMEM((32, BS), jnp.int32),
            pltpu.VMEM((8, BS), jnp.int32),
            pltpu.SMEM((32, BS), jnp.int32),
            pltpu.SMEM((8, BS), jnp.int32),
            pltpu.VMEM((2, 32, 2, 64, BS), BF16),
            pltpu.VMEM((64, 64, BS), BF16),
            pltpu.VMEM((64, 64, BS), BF16),
            pltpu.VMEM((3, 32, 8, BS), F32),
            pltpu.SemaphoreType.DMA((8,)),
            pltpu.SemaphoreType.DMA((COPIES,)),
            pltpu.SemaphoreType.DMA((COPIES,)),
        ],
        compiler_params=pltpu.CompilerParams(
            collective_id=0, has_side_effects=True, vmem_limit_bytes=60 << 20
        ),
    )(
        pattern, density, holder.reshape(1, 32), slot_index.reshape(1, 32),
        atom_index.reshape(1, 32), derivative,
    )


def solution(mesh):
    split = Mesh(mesh.devices.reshape(4, 4, 4, 2), ("layer", "z", "y", "col"))
    every = ("layer", "z", "y", "col")
    return jax.shard_map(
        shards,
        mesh=split,
        in_specs=(
            P(("z", "y"), "col"),
            P(("z", "y"), "col"),
            P(every, None),
            P(every),
            P(every),
            P(every, None, None, None),
        ),
        out_specs=P(None, every),
        check_vma=False,
    )
```

```python
import jax
import jax.numpy as jnp
from jax import lax
from jax.experimental import pallas as pl
from jax.experimental.pallas import tpu as pltpu
from jax.sharding import Mesh, PartitionSpec as P

BS = 128
ATOM_DEV = 8
CHUNKS = 4
WIDE = 256
F32 = jnp.float32
BF16 = jnp.bfloat16
MESH = pl.DeviceIdType.MESH
COPIES = 242


class Links:
    def __init__(self, place, send_sems, recv_sems):
        self.place, self.send_sems, self.recv_sems = place, send_sems, recv_sems
        self.started = []
        self.count = 0

    def copy(self, src, dst, axis, step):
        length = 2 if axis == "col" else 4
        return self.to(src, dst, {axis: lax.rem(self.place[axis] + step + length, length)})

    def to(self, src, dst, device):
        number, self.count = self.count, self.count + 1
        made = pltpu.make_async_remote_copy(
            src_ref=src,
            dst_ref=dst,
            send_sem=self.send_sems.at[number],
            recv_sem=self.recv_sems.at[number],
            device_id=device,
            device_id_type=MESH,
        )
        made.start()
        self.started.append(made)
        return made


class Ring:
    def __init__(self, links, axis, slot):
        self.links, self.axis, self.slot = links, axis, slot
        self.own = links.place[axis]

    def start(self):
        mine = self.slot(self.own)
        self.up = self.links.copy(mine, mine, self.axis, 1)
        self.down = self.links.copy(mine, mine, self.axis, -1)

    def forward(self):
        half = self.slot(self.own).shape[0] // 2
        self.up.wait_recv()
        lower = self.slot(lax.rem(self.own + 3, 4)).at[pl.ds(0, half)]
        self.up_half = self.links.copy(lower, lower, self.axis, 1)
        self.down.wait_recv()
        upper = self.slot(lax.rem(self.own + 1, 4)).at[pl.ds(half, half)]
        self.down_half = self.links.copy(upper, upper, self.axis, -1)

    def finish(self):
        self.up_half.wait_recv()
        self.down_half.wait_recv()


def purify_kernel(
    pattern, density, targets_row, slots_row, atoms_row, derivative, forces,
    rows_in, cols_in, own_in, left, left_send, right, square, part, sums_send, sums_recv, cube_send, cube_recv, pure, held_low, held_high,
    der, asked_send, asked_recv, asked_rows, spots, asked, spot_of, picked, arrived_low, arrived_high, contrib,
    in_sems, send_sems, recv_sems,
):
    held, arrived = (held_low, held_high), (arrived_low, arrived_high)
    x, z, y, c = (lax.axis_index(a) for a in ("layer", "z", "y", "col"))
    place = {"layer": x, "z": z, "y": y, "col": c}
    links = Links(place, send_sems, recv_sems)
    subs = [lax.rem(x + n, 4) for n in range(4)]
    load_rows = [
        pltpu.make_async_copy(
            density.at[pl.ds(pl.multiple_of(subs[n] * BS, BS), BS), :], rows_in.at[n], in_sems.at[n]
        )
        for n in range(2)
    ]
    load_cols = pltpu.make_async_copy(
        density.at[:, pl.ds(pl.multiple_of(x * 1024, 1024), 1024)], cols_in, in_sems.at[7]
    )
    for made in load_rows:
        made.start()
    load_cols.start()
    load_own = [
        pltpu.make_async_copy(
            density.at[:, pl.ds(pl.multiple_of(h * 2048 + y * 512, 512), 512)],
            own_in.at[h], in_sems.at[5 + h],
        )
        for h in range(2)
    ]
    for made in load_own:
        made.start()
    load_der = pltpu.make_async_copy(derivative, der, in_sems.at[2])
    load_der.start()
    barrier = pltpu.get_barrier_semaphore()
    hops = (0, 1, 2, 1)
    others = [(dz, dy, dc) for dz in range(4) for dy in range(4) for dc in range(2)][1:]
    others.sort(key=lambda d: -hops[d[0]] - hops[d[1]])

    def device(dz, dy, dc):
        return {"z": lax.rem(z + dz, 4), "y": lax.rem(y + dy, 4), "col": lax.rem(c + dc, 2)}

    def holder_of(at):
        return at["z"] * 8 + at["y"] * 2 + at["col"]

    me = z * 8 + y * 2 + c
    greeted = [device(*d) for d in others] + [{"layer": lax.rem(x + step, 4)} for step in (1, 2, 3)]
    for at in greeted:
        pl.semaphore_signal(barrier, inc=1, device_id=at, device_id_type=MESH)

    across = lax.broadcasted_iota(jnp.int32, (32, 32), 1)
    down = lax.broadcasted_iota(jnp.int32, (32, 32), 0)

    def column(row):
        return jnp.sum(jnp.where(down == across, row, 0), axis=1, keepdims=True)

    earlier = (column(targets_row[...]) == targets_row[...]) & (down < across)
    spot = 2 * targets_row[...] + jnp.sum(jnp.where(earlier, 1, 0), axis=0, keepdims=True)
    spots[...] = jnp.zeros_like(spots)
    spots[0:1, 0:32] = spot
    lane = lax.broadcasted_iota(jnp.int32, (32, BS), 1)
    table = jnp.zeros((32, BS), jnp.int32)
    for k in range(2):
        mine = jnp.where(spot == 2 * down + k, slots_row[...], 0)
        table = jnp.where(lane == k, jnp.sum(mine, axis=1, keepdims=True), table)
    asked_send[...] = jnp.broadcast_to(table[:, None, :], asked_send.shape)
    asked_recv[me] = asked_send[me]

    def kept(row_block, col_block):
        inside = pattern[row_block, col_block] == 1
        return inside | ((z * 4 + y) * 4 + row_block == c * 32 + col_block)

    def over(step):
        return lax.rem(y + step, 4)

    brought = {}

    def bring(step, n):
        brought[step, n] = links.copy(
            left_send.at[n, over(-step % 4)], left.at[c, y, subs[n]], "y", -step
        )

    for n in range(2):
        load_rows[n].wait()
        for b in range(32):
            block = rows_in[n, :, b * BS : (b + 1) * BS]
            block = jnp.where(kept(subs[n], b), block, jnp.zeros_like(block))
            lane = (b // 16) * 512 + (b % 4) * BS
            left_send[n, (b % 16) // 4, :, lane : lane + BS] = block
        if n == 0:
            pl.semaphore_wait(barrier, len(greeted))
        bring(3, n)
        bring(1, n)
    bring(2, 0)
    bring(2, 1)

    load_cols.wait()
    for b in range(8):
        for r in range(4):
            block = cols_in[r * BS : (r + 1) * BS, b * BS : (b + 1) * BS]
            block = jnp.where(kept(r, x * 8 + b), block, jnp.zeros_like(block))
            lane = (b % 2) * BS
            right[b // 2, z, r * BS : (r + 1) * BS, lane : lane + BS] = block
    requests = []
    for d in others:
        at = device(*d)
        requests.append(links.to(asked_send.at[holder_of(at)], asked_recv.at[me], at))
    rights = [
        [links.copy(right.at[j, z], right.at[j, z], "z", step) for step in (1, -1, 2)]
        for j in range(CHUNKS)
    ]

    for made in load_own:
        made.wait()
    for h in range(2):
        for r in range(4):
            for w in range(4):
                block = own_in[h, r * BS : (r + 1) * BS, w * BS : (w + 1) * BS]
                block = jnp.where(kept(r, h * 16 + y * 4 + w), block, jnp.zeros_like(block))
                lane = h * 512 + w * BS
                left[c, y, r, :, lane : lane + BS] = block
    crossed = {0: [links.copy(left.at[c, y], left.at[c, y], "col", 1)], 1: [], 2: [], 3: []}
    passed = {}

    def cross(step, away):
        piece = left.at[c, over(step), subs[away]]
        crossed[step].append(links.copy(piece, piece, "col", 1))

    def spread(step, n):
        brought[step, n].wait_recv()
        piece = left.at[c, over(step), subs[n]]
        passed[step, n] = links.copy(piece, piece, "layer", 1 - 2 * n)
        cross(step, n)

    def took(step, n):
        passed[step, n].wait_recv()
        cross(step, 3 - n)

    def complete(*steps):
        for step in steps:
            for made in crossed[step]:
                made.wait_recv()

    def multiply(j, factor, panels, half):
        height = 512 if half is None else 256
        base = 256 * (half or 0)

        def panel(turn, carry):
            i = jnp.where(turn == 0, panels[0], panels[1])
            d = lax.rem(y + jnp.where(i == 0, 2, jnp.where(i == 1, 1, jnp.where(i == 2, 3, 0))), 4)
            total = jnp.zeros((height, WIDE), F32)
            for k in range(2):
                if half is None:
                    rows = left[k, d]
                else:
                    rows = left[k, d, :, 64 * half : 64 * half + 64, :]
                total += jnp.dot(
                    rows.reshape(height, 1024),
                    factor[j, 2 * k : 2 * k + 2].reshape(1024, WIDE),
                    preferred_element_type=F32,
                )
            part[j, i, base : base + height] = total
            return carry

        lax.fori_loop(0, 2, panel, 0)

    class Sums:
        def __init__(self, j, half, factor, sent, received):
            self.j, self.half, self.factor = j, half, factor
            self.sent, self.received, self.made = sent, received, {}
            self.low = 256 * (half or 0)
            self.size = 256 if half is None else 128

        def own(self, i, upper):
            start = self.low + self.size * upper
            return part[self.j, i, start : start + self.size]

        def send(self, n, value, step):
            self.sent[n] = value.astype(BF16)
            self.made[n] = links.copy(self.sent.at[n], self.received.at[n], "y", step)

        def far(self):
            multiply(self.j, self.factor, (0, 3), self.half)
            self.send(0, self.own(0, 0), 1)
            self.send(1, self.own(0, 1), -1)

        def near(self):
            multiply(self.j, self.factor, (1, 2), self.half)
            self.send(2, self.own(1, 1), 1)
            self.send(3, self.own(2, 0), -1)

        def combine(self):
            self.made[0].wait_recv()
            self.send(4, self.own(1, 0) + self.received[0].astype(F32), 1)
            self.made[1].wait_recv()
            self.send(5, self.own(2, 1) + self.received[1].astype(F32), -1)

        def result(self):
            for n in (2, 3, 4, 5):
                self.made[n].wait_recv()
            return [
                self.own(3, h) + self.received[a].astype(F32) + self.received[b].astype(F32)
                for h, (a, b) in enumerate(((3, 4), (2, 5)))
            ]

    squares = [Sums(j, None, right, sums_send.at[j], sums_recv.at[j]) for j in range(CHUNKS)]
    cubes = [
        [
            Sums(j, half, square, cube_send.at[half, j], cube_recv.at[half, j])
            for j in range(CHUNKS)
        ]
        for half in range(2)
    ]
    gathers = [Ring(links, "z", lambda s, j=j: square.at[j, s]) for j in range(CHUNKS)]
    handed = [[], []]

    def squared(j):
        for h, value in enumerate(squares[j].result()):
            square[j, z, h * 256 : (h + 1) * 256] = value.astype(BF16)
        gathers[j].start()

    gone = set()

    def second(half, j):
        if j not in gone:
            gathers[j].finish()
            gone.add(j)
        cubes[half][j].far()
        cubes[half][j].near()

    def purified(half, j):
        for h, value in enumerate(cubes[half][j].result()):
            for r in range(2):
                row = 2 * h + r
                start = row * BS + 64 * half
                for b in range(2):
                    lanes = slice(b * BS, (b + 1) * BS)
                    own = square[j, z, start : start + 64, lanes].astype(F32)
                    block = 3.0 * own - 2.0 * value[64 * r : 64 * r + 64, lanes]
                    block = jnp.where(kept(row, x * 8 + j * 2 + b), block, jnp.zeros_like(block))
                    pure[half, j, row, b] = block.astype(BF16)
        where = x * 8 + j * 2
        for step in (1, 2, 3):
            to = lax.rem(x + step, 4)
            handed[half].append(
                links.copy(pure.at[half, j, to], held[half].at[pl.ds(where, 2)], "layer", step)
            )
        for b in range(2):
            held[half][where + b] = pure[half, j, x, b]

    fetches = [[], []]

    def fetch(half):
        for made in handed[half]:
            made.wait_recv()
        for d in others:
            at = device(*d)
            to = holder_of(at)
            for k in range(2):
                picked[half, to, k] = held[half][asked[to, k]]
            fetches[half].append(
                links.to(picked.at[half, to], arrived[half].at[pl.ds(2 * me, 2)], at)
            )
        for k in range(2):
            arrived[half][2 * me + k] = held[half][asked[me, k]]

    def contract(half):
        for made in fetches[half]:
            made.wait_recv()

        def entry(e, carry):
            block = arrived[half][spot_of[0, e]].astype(F32)
            for k in range(3):
                terms = block * der[e, k, 64 * half : 64 * half + 64, :].astype(F32)
                total = jnp.sum(terms.reshape(8, 8, BS), axis=0)
                contrib[k, e] = total if half == 0 else contrib[k, e] + total
            return carry

        lax.fori_loop(0, 32, entry, 0, unroll=4)

    def righted(j):
        for made in rights[j]:
            made.wait_recv()

    spread(3, 0)
    spread(1, 0)
    spread(3, 1)
    spread(1, 1)
    took(3, 0)
    spread(2, 0)
    took(3, 1)
    took(1, 0)
    spread(2, 1)
    for made in requests:
        made.wait_recv()
    asked_rows[...] = asked_recv[:, 0, :]
    tables = [
        pltpu.make_async_copy(asked_rows, asked, in_sems.at[3]),
        pltpu.make_async_copy(spots, spot_of, in_sems.at[4]),
    ]
    for made in tables:
        made.start()
    took(1, 1)
    took(2, 0)
    for made in tables:
        made.wait()
    complete(0, 3, 1)
    for j in (0, 1):
        righted(j)
        squares[j].near()
    took(2, 1)
    complete(2)
    squares[0].far()
    squares[1].far()
    squares[0].combine()
    squares[1].combine()
    righted(2)
    squares[2].near()
    squares[2].far()
    squared(0)
    squared(1)
    righted(3)
    squares[3].near()
    squares[3].far()
    squares[2].combine()
    gathers[0].forward()
    squares[3].combine()
    gathers[1].forward()
    squared(2)
    second(0, 0)
    cubes[0][0].combine()
    second(1, 0)
    squared(3)
    second(0, 1)
    cubes[1][0].combine()
    gathers[2].forward()
    second(1, 1)
    cubes[0][1].combine()
    purified(0, 0)
    purified(1, 0)
    gathers[3].forward()
    cubes[1][1].combine()
    second(0, 2)
    purified(0, 1)
    second(0, 3)
    purified(1, 1)
    cubes[0][2].combine()
    cubes[0][3].combine()
    second(1, 2)
    second(1, 3)
    purified(0, 2)
    purified(0, 3)
    cubes[1][2].combine()
    cubes[1][3].combine()
    purified(1, 2)
    fetch(0)
    purified(1, 3)
    load_der.wait()
    fetch(1)
    contract(0)
    contract(1)
    atoms = lax.broadcasted_iota(jnp.int32, (32, ATOM_DEV), 1)
    atom_hot = jnp.where(column(atoms_row[...]) == atoms, 1.0, 0.0).astype(F32)
    for k in range(3):
        terms = jnp.sum(jnp.sum(contrib[k], axis=1), axis=1, keepdims=True)
        forces[k : k + 1, :] = -2.0 * jnp.sum(terms * atom_hot, axis=0, keepdims=True)
    for made in links.started:
        made.wait_send()
    assert links.count == COPIES, links.count


def shards(density, pattern, holder, slot_index, atom_index, derivative):
    vmem = pl.BlockSpec(memory_space=pltpu.VMEM)
    hbm = pl.BlockSpec(memory_space=pl.ANY)
    return pl.pallas_call(
        purify_kernel,
        out_shape=jax.ShapeDtypeStruct((3, ATOM_DEV), F32),
        in_specs=[pl.BlockSpec(memory_space=pltpu.SMEM), hbm, vmem, vmem, vmem, hbm],
        out_specs=vmem,
        scratch_shapes=[
            pltpu.VMEM((2, BS, 4096), BF16),
            pltpu.VMEM((512, 1024), BF16),
            pltpu.VMEM((2, 512, 512), BF16),
            pltpu.VMEM((2, 4, 4, BS, 1024), BF16),
            pltpu.VMEM((2, 4, BS, 1024), BF16),
            pltpu.VMEM((CHUNKS, 4, 512, WIDE), BF16),
            pltpu.VMEM((CHUNKS, 4, 512, WIDE), BF16),
            pltpu.VMEM((CHUNKS, 4, 512, WIDE), F32),
            pltpu.VMEM((CHUNKS, 6, 256, WIDE), BF16),
            pltpu.VMEM((CHUNKS, 6, 256, WIDE), BF16),
            pltpu.VMEM((2, CHUNKS, 6, BS, WIDE), BF16),
            pltpu.VMEM((2, CHUNKS, 6, BS, WIDE), BF16),
            pltpu.VMEM((2, CHUNKS, 4, 2, 64, BS), BF16),
            pltpu.VMEM((32, 64, BS), BF16),
            pltpu.VMEM((32, 64, BS), BF16),
            pltpu.VMEM((32, 3, BS, BS), BF16),
            pltpu.VMEM((32, 8, BS), jnp.int32),
            pltpu.VMEM((32, 8, BS), jnp.int32),
            pltpu.VMEM((32, BS), jnp.int32),
            pltpu.VMEM((8, BS), jnp.int32),
            pltpu.SMEM((32, BS), jnp.int32),
            pltpu.SMEM((8, BS), jnp.int32),
            pltpu.VMEM((2, 32, 2, 64, BS), BF16),
            pltpu.VMEM((64, 64, BS), BF16),
            pltpu.VMEM((64, 64, BS), BF16),
            pltpu.VMEM((3, 32, 8, BS), F32),
            pltpu.SemaphoreType.DMA((8,)),
            pltpu.SemaphoreType.DMA((COPIES,)),
            pltpu.SemaphoreType.DMA((COPIES,)),
        ],
        compiler_params=pltpu.CompilerParams(
            collective_id=0, has_side_effects=True, vmem_limit_bytes=60 << 20
        ),
    )(
        pattern, density, holder.reshape(1, 32), slot_index.reshape(1, 32),
        atom_index.reshape(1, 32), derivative,
    )


def solution(mesh):
    split = Mesh(mesh.devices.reshape(4, 4, 4, 2), ("layer", "z", "y", "col"))
    every = ("layer", "z", "y", "col")
    return jax.shard_map(
        shards,
        mesh=split,
        in_specs=(
            P(("z", "y"), "col"),
            P(("z", "y"), "col"),
            P(every, None),
            P(every),
            P(every),
            P(every, None, None, None),
        ),
        out_specs=P(None, every),
        check_vma=False,
    )
```

```python
import jax
import jax.numpy as jnp
from jax import lax
from jax.experimental import pallas as pl
from jax.experimental.pallas import tpu as pltpu
from jax.sharding import Mesh, PartitionSpec as P

BS = 128
ATOM_DEV = 8
CHUNKS = 4
WIDE = 256
F32 = jnp.float32
BF16 = jnp.bfloat16
MESH = pl.DeviceIdType.MESH
COPIES = 242


class Links:
    def __init__(self, place, send_sems, recv_sems):
        self.place, self.send_sems, self.recv_sems = place, send_sems, recv_sems
        self.started = []
        self.count = 0

    def copy(self, src, dst, axis, step):
        length = 2 if axis == "col" else 4
        return self.to(src, dst, {axis: lax.rem(self.place[axis] + step + length, length)})

    def to(self, src, dst, device):
        number, self.count = self.count, self.count + 1
        made = pltpu.make_async_remote_copy(
            src_ref=src,
            dst_ref=dst,
            send_sem=self.send_sems.at[number],
            recv_sem=self.recv_sems.at[number],
            device_id=device,
            device_id_type=MESH,
        )
        made.start()
        self.started.append(made)
        return made


class Ring:
    def __init__(self, links, axis, slot):
        self.links, self.axis, self.slot = links, axis, slot
        self.own = links.place[axis]

    def start(self):
        mine = self.slot(self.own)
        self.up = self.links.copy(mine, mine, self.axis, 1)
        self.down = self.links.copy(mine, mine, self.axis, -1)

    def forward(self):
        half = self.slot(self.own).shape[0] // 2
        self.up.wait_recv()
        lower = self.slot(lax.rem(self.own + 3, 4)).at[pl.ds(0, half)]
        self.up_half = self.links.copy(lower, lower, self.axis, 1)
        self.down.wait_recv()
        upper = self.slot(lax.rem(self.own + 1, 4)).at[pl.ds(half, half)]
        self.down_half = self.links.copy(upper, upper, self.axis, -1)

    def finish(self):
        self.up_half.wait_recv()
        self.down_half.wait_recv()


def purify_kernel(
    pattern, density, targets_row, slots_row, atoms_row, derivative, forces,
    rows_in, cols_in, own_in, left, left_send, right, square, part, sums_send, sums_recv, cube_send, cube_recv, pure, held_low, held_high,
    der, asked_send, asked_recv, asked_rows, spots, asked, spot_of, picked, arrived_low, arrived_high, contrib,
    in_sems, send_sems, recv_sems,
):
    held, arrived = (held_low, held_high), (arrived_low, arrived_high)
    x, z, y, c = (lax.axis_index(a) for a in ("layer", "z", "y", "col"))
    place = {"layer": x, "z": z, "y": y, "col": c}
    links = Links(place, send_sems, recv_sems)
    subs = [lax.rem(x + n, 4) for n in range(4)]
    load_rows = [
        pltpu.make_async_copy(
            density.at[pl.ds(pl.multiple_of(subs[n] * BS, BS), BS), :], rows_in.at[n], in_sems.at[n]
        )
        for n in range(2)
    ]
    load_cols = pltpu.make_async_copy(
        density.at[:, pl.ds(pl.multiple_of(x * 1024, 1024), 1024)], cols_in, in_sems.at[7]
    )
    for made in load_rows:
        made.start()
    load_cols.start()
    load_own = [
        pltpu.make_async_copy(
            density.at[:, pl.ds(pl.multiple_of(h * 2048 + y * 512, 512), 512)],
            own_in.at[h], in_sems.at[5 + h],
        )
        for h in range(2)
    ]
    for made in load_own:
        made.start()
    load_der = pltpu.make_async_copy(derivative, der, in_sems.at[2])
    load_der.start()
    barrier = pltpu.get_barrier_semaphore()
    hops = (0, 1, 2, 1)
    others = [(dz, dy, dc) for dz in range(4) for dy in range(4) for dc in range(2)][1:]
    others.sort(key=lambda d: -hops[d[0]] - hops[d[1]])

    def device(dz, dy, dc):
        return {"z": lax.rem(z + dz, 4), "y": lax.rem(y + dy, 4), "col": lax.rem(c + dc, 2)}

    def holder_of(at):
        return at["z"] * 8 + at["y"] * 2 + at["col"]

    me = z * 8 + y * 2 + c
    greeted = [{"col": 1 - c}]
    for axis in ("y", "z", "layer"):
        greeted += [{axis: lax.rem(place[axis] + step, 4)} for step in (1, 2, 3)]
    for at in greeted:
        pl.semaphore_signal(barrier, inc=1, device_id=at, device_id_type=MESH)

    across = lax.broadcasted_iota(jnp.int32, (32, 32), 1)
    down = lax.broadcasted_iota(jnp.int32, (32, 32), 0)

    def column(row):
        return jnp.sum(jnp.where(down == across, row, 0), axis=1, keepdims=True)

    earlier = (column(targets_row[...]) == targets_row[...]) & (down < across)
    spot = 2 * targets_row[...] + jnp.sum(jnp.where(earlier, 1, 0), axis=0, keepdims=True)
    spots[...] = jnp.zeros_like(spots)
    spots[0:1, 0:32] = spot
    lane = lax.broadcasted_iota(jnp.int32, (32, BS), 1)
    table = jnp.zeros((32, BS), jnp.int32)
    for k in range(2):
        mine = jnp.where(spot == 2 * down + k, slots_row[...], 0)
        table = jnp.where(lane == k, jnp.sum(mine, axis=1, keepdims=True), table)
    asked_send[...] = jnp.broadcast_to(table[:, None, :], asked_send.shape)
    asked_recv[me] = asked_send[me]

    def kept(row_block, col_block):
        inside = pattern[row_block, col_block] == 1
        return inside | ((z * 4 + y) * 4 + row_block == c * 32 + col_block)

    def over(step):
        return lax.rem(y + step, 4)

    brought = {}

    def bring(step, n):
        brought[step, n] = links.copy(
            left_send.at[n, over(-step % 4)], left.at[c, y, subs[n]], "y", -step
        )

    for n in range(2):
        load_rows[n].wait()
        for b in range(32):
            block = rows_in[n, :, b * BS : (b + 1) * BS]
            block = jnp.where(kept(subs[n], b), block, jnp.zeros_like(block))
            lane = (b // 16) * 512 + (b % 4) * BS
            left_send[n, (b % 16) // 4, :, lane : lane + BS] = block
        if n == 0:
            pl.semaphore_wait(barrier, len(greeted))
        bring(3, n)
        bring(1, n)
    bring(2, 0)
    bring(2, 1)

    load_cols.wait()
    for b in range(8):
        for r in range(4):
            block = cols_in[r * BS : (r + 1) * BS, b * BS : (b + 1) * BS]
            block = jnp.where(kept(r, x * 8 + b), block, jnp.zeros_like(block))
            lane = (b % 2) * BS
            right[b // 2, z, r * BS : (r + 1) * BS, lane : lane + BS] = block
    rights = [
        [links.copy(right.at[j, z], right.at[j, z], "z", step) for step in (1, -1, 2)]
        for j in range(CHUNKS)
    ]

    for made in load_own:
        made.wait()
    for h in range(2):
        for r in range(4):
            for w in range(4):
                block = own_in[h, r * BS : (r + 1) * BS, w * BS : (w + 1) * BS]
                block = jnp.where(kept(r, h * 16 + y * 4 + w), block, jnp.zeros_like(block))
                lane = h * 512 + w * BS
                left[c, y, r, :, lane : lane + BS] = block
    crossed = {0: [links.copy(left.at[c, y], left.at[c, y], "col", 1)], 1: [], 2: [], 3: []}
    passed = {}

    def cross(step, away):
        piece = left.at[c, over(step), subs[away]]
        crossed[step].append(links.copy(piece, piece, "col", 1))

    def spread(step, n):
        brought[step, n].wait_recv()
        piece = left.at[c, over(step), subs[n]]
        passed[step, n] = links.copy(piece, piece, "layer", 1 - 2 * n)
        cross(step, n)

    def took(step, n):
        passed[step, n].wait_recv()
        cross(step, 3 - n)

    def complete(*steps):
        for step in steps:
            for made in crossed[step]:
                made.wait_recv()

    def multiply(j, factor, panels, half):
        height = 512 if half is None else 256
        base = 256 * (half or 0)

        def panel(turn, carry):
            i = jnp.where(turn == 0, panels[0], panels[1])
            d = lax.rem(y + jnp.where(i == 0, 2, jnp.where(i == 1, 1, jnp.where(i == 2, 3, 0))), 4)
            total = jnp.zeros((height, WIDE), F32)
            for k in range(2):
                if half is None:
                    rows = left[k, d]
                else:
                    rows = left[k, d, :, 64 * half : 64 * half + 64, :]
                total += jnp.dot(
                    rows.reshape(height, 1024),
                    factor[j, 2 * k : 2 * k + 2].reshape(1024, WIDE),
                    preferred_element_type=F32,
                )
            part[j, i, base : base + height] = total
            return carry

        lax.fori_loop(0, 2, panel, 0)

    class Sums:
        def __init__(self, j, half, factor, sent, received):
            self.j, self.half, self.factor = j, half, factor
            self.sent, self.received, self.made = sent, received, {}
            self.low = 256 * (half or 0)
            self.size = 256 if half is None else 128

        def own(self, i, upper):
            start = self.low + self.size * upper
            return part[self.j, i, start : start + self.size]

        def send(self, n, value, step):
            self.sent[n] = value.astype(BF16)
            self.made[n] = links.copy(self.sent.at[n], self.received.at[n], "y", step)

        def far(self):
            multiply(self.j, self.factor, (0, 3), self.half)
            self.send(0, self.own(0, 0), 1)
            self.send(1, self.own(0, 1), -1)

        def near(self):
            multiply(self.j, self.factor, (1, 2), self.half)
            self.send(2, self.own(1, 1), 1)
            self.send(3, self.own(2, 0), -1)

        def combine(self):
            self.made[0].wait_recv()
            self.send(4, self.own(1, 0) + self.received[0].astype(F32), 1)
            self.made[1].wait_recv()
            self.send(5, self.own(2, 1) + self.received[1].astype(F32), -1)

        def result(self):
            for n in (2, 3, 4, 5):
                self.made[n].wait_recv()
            return [
                self.own(3, h) + self.received[a].astype(F32) + self.received[b].astype(F32)
                for h, (a, b) in enumerate(((3, 4), (2, 5)))
            ]

    squares = [Sums(j, None, right, sums_send.at[j], sums_recv.at[j]) for j in range(CHUNKS)]
    cubes = [
        [
            Sums(j, half, square, cube_send.at[half, j], cube_recv.at[half, j])
            for j in range(CHUNKS)
        ]
        for half in range(2)
    ]
    gathers = [Ring(links, "z", lambda s, j=j: square.at[j, s]) for j in range(CHUNKS)]
    handed = [[], []]

    def squared(j):
        for h, value in enumerate(squares[j].result()):
            square[j, z, h * 256 : (h + 1) * 256] = value.astype(BF16)
        gathers[j].start()

    gone = set()

    def second(half, j):
        if j not in gone:
            gathers[j].finish()
            gone.add(j)
        cubes[half][j].far()
        cubes[half][j].near()

    def purified(half, j):
        for h, value in enumerate(cubes[half][j].result()):
            for r in range(2):
                row = 2 * h + r
                start = row * BS + 64 * half
                for b in range(2):
                    lanes = slice(b * BS, (b + 1) * BS)
                    own = square[j, z, start : start + 64, lanes].astype(F32)
                    block = 3.0 * own - 2.0 * value[64 * r : 64 * r + 64, lanes]
                    block = jnp.where(kept(row, x * 8 + j * 2 + b), block, jnp.zeros_like(block))
                    pure[half, j, row, b] = block.astype(BF16)
        where = x * 8 + j * 2
        for step in (1, 2, 3):
            to = lax.rem(x + step, 4)
            handed[half].append(
                links.copy(pure.at[half, j, to], held[half].at[pl.ds(where, 2)], "layer", step)
            )
        for b in range(2):
            held[half][where + b] = pure[half, j, x, b]

    fetches = [[], []]

    def fetch(half):
        for made in handed[half]:
            made.wait_recv()
        for d in others:
            at = device(*d)
            to = holder_of(at)
            for k in range(2):
                picked[half, to, k] = held[half][asked[to, k]]
            fetches[half].append(
                links.to(picked.at[half, to], arrived[half].at[pl.ds(2 * me, 2)], at)
            )
        for k in range(2):
            arrived[half][2 * me + k] = held[half][asked[me, k]]

    def contract(half):
        for made in fetches[half]:
            made.wait_recv()

        def entry(e, carry):
            block = arrived[half][spot_of[0, e]].astype(F32)
            for k in range(3):
                terms = block * der[e, k, 64 * half : 64 * half + 64, :].astype(F32)
                total = jnp.sum(terms.reshape(8, 8, BS), axis=0)
                contrib[k, e] = total if half == 0 else contrib[k, e] + total
            return carry

        lax.fori_loop(0, 32, entry, 0, unroll=4)

    def righted(j):
        for made in rights[j]:
            made.wait_recv()

    spread(3, 0)
    spread(1, 0)
    spread(3, 1)
    spread(1, 1)
    took(3, 0)
    spread(2, 0)
    took(3, 1)
    took(1, 0)
    spread(2, 1)
    took(1, 1)
    took(2, 0)
    complete(0, 3, 1)
    for j in (0, 1):
        righted(j)
        squares[j].near()
    took(2, 1)
    complete(2)
    squares[0].far()
    squares[1].far()
    squares[0].combine()
    squares[1].combine()
    righted(2)
    squares[2].near()
    squares[2].far()
    squared(0)
    requests = []
    for d in others:
        at = device(*d)
        requests.append(links.to(asked_send.at[holder_of(at)], asked_recv.at[me], at))
    squared(1)
    righted(3)
    squares[3].near()
    squares[3].far()
    squares[2].combine()
    gathers[0].forward()
    squares[3].combine()
    gathers[1].forward()
    squared(2)
    second(0, 0)
    cubes[0][0].combine()
    second(1, 0)
    squared(3)
    second(0, 1)
    cubes[1][0].combine()
    gathers[2].forward()
    second(1, 1)
    cubes[0][1].combine()
    purified(0, 0)
    purified(1, 0)
    gathers[3].forward()
    cubes[1][1].combine()
    second(0, 2)
    purified(0, 1)
    second(0, 3)
    purified(1, 1)
    cubes[0][2].combine()
    cubes[0][3].combine()
    second(1, 2)
    second(1, 3)
    for made in requests:
        made.wait_recv()
    asked_rows[...] = asked_recv[:, 0, :]
    tables = [
        pltpu.make_async_copy(asked_rows, asked, in_sems.at[3]),
        pltpu.make_async_copy(spots, spot_of, in_sems.at[4]),
    ]
    for made in tables:
        made.start()
    purified(0, 2)
    purified(0, 3)
    cubes[1][2].combine()
    cubes[1][3].combine()
    purified(1, 2)
    for made in tables:
        made.wait()
    fetch(0)
    purified(1, 3)
    load_der.wait()
    fetch(1)
    contract(0)
    contract(1)
    atoms = lax.broadcasted_iota(jnp.int32, (32, ATOM_DEV), 1)
    atom_hot = jnp.where(column(atoms_row[...]) == atoms, 1.0, 0.0).astype(F32)
    for k in range(3):
        terms = jnp.sum(jnp.sum(contrib[k], axis=1), axis=1, keepdims=True)
        forces[k : k + 1, :] = -2.0 * jnp.sum(terms * atom_hot, axis=0, keepdims=True)
    for made in links.started:
        made.wait_send()
    assert links.count == COPIES, links.count


def shards(density, pattern, holder, slot_index, atom_index, derivative):
    vmem = pl.BlockSpec(memory_space=pltpu.VMEM)
    hbm = pl.BlockSpec(memory_space=pl.ANY)
    return pl.pallas_call(
        purify_kernel,
        out_shape=jax.ShapeDtypeStruct((3, ATOM_DEV), F32),
        in_specs=[pl.BlockSpec(memory_space=pltpu.SMEM), hbm, vmem, vmem, vmem, hbm],
        out_specs=vmem,
        scratch_shapes=[
            pltpu.VMEM((2, BS, 4096), BF16),
            pltpu.VMEM((512, 1024), BF16),
            pltpu.VMEM((2, 512, 512), BF16),
            pltpu.VMEM((2, 4, 4, BS, 1024), BF16),
            pltpu.VMEM((2, 4, BS, 1024), BF16),
            pltpu.VMEM((CHUNKS, 4, 512, WIDE), BF16),
            pltpu.VMEM((CHUNKS, 4, 512, WIDE), BF16),
            pltpu.VMEM((CHUNKS, 4, 512, WIDE), F32),
            pltpu.VMEM((CHUNKS, 6, 256, WIDE), BF16),
            pltpu.VMEM((CHUNKS, 6, 256, WIDE), BF16),
            pltpu.VMEM((2, CHUNKS, 6, BS, WIDE), BF16),
            pltpu.VMEM((2, CHUNKS, 6, BS, WIDE), BF16),
            pltpu.VMEM((2, CHUNKS, 4, 2, 64, BS), BF16),
            pltpu.VMEM((32, 64, BS), BF16),
            pltpu.VMEM((32, 64, BS), BF16),
            pltpu.VMEM((32, 3, BS, BS), BF16),
            pltpu.VMEM((32, 8, BS), jnp.int32),
            pltpu.VMEM((32, 8, BS), jnp.int32),
            pltpu.VMEM((32, BS), jnp.int32),
            pltpu.VMEM((8, BS), jnp.int32),
            pltpu.SMEM((32, BS), jnp.int32),
            pltpu.SMEM((8, BS), jnp.int32),
            pltpu.VMEM((2, 32, 2, 64, BS), BF16),
            pltpu.VMEM((64, 64, BS), BF16),
            pltpu.VMEM((64, 64, BS), BF16),
            pltpu.VMEM((3, 32, 8, BS), F32),
            pltpu.SemaphoreType.DMA((8,)),
            pltpu.SemaphoreType.DMA((COPIES,)),
            pltpu.SemaphoreType.DMA((COPIES,)),
        ],
        compiler_params=pltpu.CompilerParams(
            collective_id=0, has_side_effects=True, vmem_limit_bytes=60 << 20
        ),
    )(
        pattern, density, holder.reshape(1, 32), slot_index.reshape(1, 32),
        atom_index.reshape(1, 32), derivative,
    )


def solution(mesh):
    split = Mesh(mesh.devices.reshape(4, 4, 4, 2), ("layer", "z", "y", "col"))
    every = ("layer", "z", "y", "col")
    return jax.shard_map(
        shards,
        mesh=split,
        in_specs=(
            P(("z", "y"), "col"),
            P(("z", "y"), "col"),
            P(every, None),
            P(every),
            P(every),
            P(every, None, None, None),
        ),
        out_specs=P(None, every),
        check_vma=False,
    )
```
